32 devices in a mesh: groups: 2 (over x), cx: 16 (over z, y, core).
Axes of the slice: x: 2, y: 2, z: 4, core: 2. Of those that a mesh axis runs over, the one named last changes fastest.
Arguments:
- displacements: bfloat16 [512, 3, 5120], P(('groups', 'cx')), parts along dimension 0, may hold values from -6 to 6
- forces: bfloat16 [512, 3, 5120], P(('groups', 'cx')), parts along dimension 0, may hold values from -6 to 6
- phi: bfloat16 [160, 14, 192, 192], P(('groups', 'cx')), parts along dimension 0, may hold values from -0.125 to 0.125
- neighbours: int32 [80, 14], P('cx'), may hold values from 0 to 79, as said below
- cluster_atoms: int32 [80, 64], P('cx'), may hold values from 0 to 5119, as said below
- config_order: int32 [512], P('groups'), parts along dimension 0, may hold values from 0 to 255, each once
- weights: float32 [512], P('groups'), parts along dimension 0, may hold values from 0.02 to 0.3
Outputs:
- residual: bfloat16 [160, 192, 256], P(('groups', 'cx')), parts along dimension 0
- gradient: bfloat16 [160, 14, 192, 192], P(('groups', 'cx')), parts along dimension 0
The draws below stay inside these ranges and needn't reach their ends.
There are 2 independent parts, one for each index of `groups`. The reference program is written for one: setup_inputs(seed, part) draws one part's arguments, and reference() takes and returns one part's arrays. A program takes and returns all parts, laid end to end along the dimension named above; an argument that names none is the same for every part. Nothing has to cross between parts.
Inputs may be any that keep to these rules, and one draw needn't show every extreme that they name: `neighbours`: cluster c lies in layer c // 5 of 16 periodic layers; its 14 blocks name distinct clusters of its own layer and the two layers beside it, wrapping at the ends. `cluster_atoms`: the clusters of layer j hold the atoms 5 * 64 * j to 5 * 64 * (j + 1) - 1, each once. `config_order`: each ensemble index once.
All inputs are finite; a program needn't handle non-finite values.
Results may differ from the reference program's by a relative error of at most 0.0085.
Values may be sent and summed in bfloat16 or wider, within the bound.
No kernel may reach another device: no remote copies, remote signals or barrier semaphores. Data moves between devices by JAX's collectives and lax.ppermute only.
A program may use at most 128 MiB of HBM per device.

```python
import math
import jax
import jax.numpy as jnp
from jax import lax

CONFIGS = 256
ATOMS = 64
LAYER = 5
BLOCKS = 14
DOF = 192
CLUSTERS = 80
NATOM = 5120


def draw_neighbours(key, part):
    layers = CLUSTERS // LAYER
    keys = jax.random.split(jax.random.fold_in(key, 11), CLUSTERS)

    def pick_one(subkey):
        return jax.random.permutation(subkey, 3 * LAYER)[:BLOCKS]
    picks = jax.vmap(pick_one)(keys).astype(jnp.int32)
    layer_of = (jnp.arange(CLUSTERS, dtype=jnp.int32) // LAYER)[:, None]
    offset = picks // LAYER - 1
    within = picks % LAYER
    return ((layer_of + offset + layers) % layers * LAYER + within).astype(jnp.int32)


def draw_cluster_atoms(key, part):
    layers = CLUSTERS // LAYER
    keys = jax.random.split(jax.random.fold_in(key, 23), layers)

    def layer_atoms(subkey):
        return jax.random.permutation(subkey, LAYER * ATOMS).astype(jnp.int32)
    picks = jax.vmap(layer_atoms)(keys)
    starts = (jnp.arange(layers, dtype=jnp.int32) * (LAYER * ATOMS))[:, None]
    return (picks + starts).reshape(CLUSTERS, ATOMS).astype(jnp.int32)


def levels(stream_key, dims, cuts, smallest, high):
    gain = 1.0
    for axis_at, parts in cuts:
        heights = jax.random.uniform(jax.random.fold_in(jax.random.fold_in(stream_key, 6), axis_at), (parts,), jnp.float32, smallest / len(cuts), high / len(cuts))
        gain = gain * jnp.repeat(jnp.exp(heights), dims[axis_at] // parts).reshape((-1,) + (1,) * (len(dims) - 1 - axis_at))
    return gain


def noise(key, extent, scale, reach, shards=(), held_as=jnp.bfloat16):
    result = jax.random.normal(key, extent, jnp.float32) * scale
    if len(shards) > 0:
        result = levels(key, extent, shards, -0.22, 0.18) * result
    return jnp.clip(result, min=-reach, max=reach).astype(held_as)


def setup_inputs(seed: int = 0, part: int = 0) -> dict:
    key_list = jax.random.split(jax.random.key(seed), 8)
    own_keys = jax.random.split(jax.random.fold_in(key_list[7], part), 8)
    return {
        "displacements": noise(own_keys[0], (CONFIGS, 3, NATOM), 1.0, 6.0, ((0, 16),)),
        "forces": noise(own_keys[1], (CONFIGS, 3, NATOM), 1.0, 6.0, ((0, 16),)),
        "phi": noise(own_keys[2], (CLUSTERS, BLOCKS, DOF, DOF), (BLOCKS * DOF) ** -0.5, 0.125, ((0, 16),)),
        "neighbours": draw_neighbours(jax.random.fold_in(key_list[7], 71), part),
        "cluster_atoms": draw_cluster_atoms(jax.random.fold_in(key_list[7], 71), part),
        "config_order": jax.random.permutation(own_keys[5], CONFIGS).astype(jnp.int32),
        "weights": jnp.clip(jnp.exp(jax.random.uniform(own_keys[6], (CONFIGS,), jnp.float32, math.log(0.02), math.log(0.3))), 0.02, 0.3),
    }


def arrange(field, atom_map):
    picked = jnp.take(field, atom_map.reshape(-1), axis=2)
    picked = picked.reshape(field.shape[0], 3, atom_map.shape[0], atom_map.shape[1])
    return jnp.transpose(picked, (2, 1, 3, 0)).reshape(atom_map.shape[0], 3 * atom_map.shape[1], field.shape[0])


def reference(displacements, forces, phi, neighbours, cluster_atoms, config_order, weights):
    cdisp = arrange(displacements, cluster_atoms)
    cforce = arrange(forces, cluster_atoms)
    index_all = jnp.arange(CLUSTERS, dtype=jnp.int32)

    def harm_one(cluster):
        near = jnp.take(cdisp, neighbours[cluster], axis=0).astype(jnp.float32)
        return jnp.einsum('kij,kjs->is', phi[cluster].astype(jnp.float32), near)

    harmonic = lax.map(harm_one, index_all)
    residual = (cforce.astype(jnp.float32) + harmonic).astype(jnp.bfloat16)
    match = config_order[:, None] == jnp.arange(CONFIGS, dtype=jnp.int32)[None, :]
    weight_row = jnp.sum(jnp.where(match, weights[None, :], jnp.zeros_like(weights)[None, :]), axis=1)
    wres = (residual.astype(jnp.float32) * weight_row[None, None, :]).astype(jnp.bfloat16)
    wdisp = (cdisp.astype(jnp.float32) * weight_row[None, None, :]).astype(jnp.bfloat16)

    def grad_one(cluster):
        near_disp = jnp.take(cdisp, neighbours[cluster], axis=0).astype(jnp.float32)
        near_resid = jnp.take(residual, neighbours[cluster], axis=0).astype(jnp.float32)
        first = jnp.einsum('is,kjs->kij', wres[cluster].astype(jnp.float32), near_disp)
        second = jnp.einsum('is,kjs->kij', wdisp[cluster].astype(jnp.float32), near_resid)
        return (0.5 * (first + second)).astype(jnp.bfloat16)

    gradient = lax.map(grad_one, index_all)
    return (residual, gradient)
```

```python
import jax
import jax.numpy as jnp
from jax import lax
from jax.experimental import pallas as pl
from jax.experimental.pallas import tpu as pltpu
from jax.sharding import PartitionSpec as P

BF16 = jnp.bfloat16
F32 = jnp.float32
VMEM = pltpu.VMEM
NT = (((1,), (1,)), ((), ()))


def whole(*arrays):
    return [pl.BlockSpec(memory_space=VMEM) for _ in arrays]


def params(**kw):
    return pltpu.CompilerParams(vmem_limit_bytes=48 * 1024 * 1024, **kw)


def cost(flops, nbytes):
    return pl.CostEstimate(flops=flops, bytes_accessed=nbytes, transcendentals=0)


def pack_kernel(disp_ref, force_ref, out1_ref, out2_ref, scratch):
    configs, parts, lanes = disp_ref.shape
    tiles = lanes // 128
    full = tiles // 2
    low = lax.broadcasted_iota(jnp.int32, (configs, 128), 1) < 64
    pieces = []
    for field, ref in enumerate((disp_ref, force_ref)):
        for s in range(configs):
            row = ref[s].astype(F32)
            for t in range(tiles):
                scratch[field, t, pl.ds(8 * s, parts), :] = row[:, 128 * t : 128 * (t + 1)]
    for field in range(2):
        pieces.append(
            [
                [scratch[field, t, pl.ds(a, configs, stride=8), :] for t in range(tiles)]
                for a in range(parts)
            ]
        )
    disp, force = pieces
    for e in range(2):
        first = e * (full + 1)

        def paired(lower, upper, e=e):
            if e == 0:
                return jnp.where(low, lower, pltpu.roll(upper, 64, 1))
            return jnp.where(low, pltpu.roll(lower, 64, 1), upper)

        for a in range(parts):
            for t in range(full):
                out1_ref[e, a * full + t] = disp[a][first + t].astype(BF16)
                out2_ref[e, a * full + t] = force[a][first + t].astype(BF16)
        base = parts * full
        out1_ref[e, base] = paired(disp[0][full], disp[1][full]).astype(BF16)
        out1_ref[e, base + 1] = paired(disp[2][full], force[2][full]).astype(BF16)
        out2_ref[e, base] = paired(force[0][full], force[1][full]).astype(BF16)


def pack(displacements, forces, width):
    configs, parts, atoms = displacements.shape
    per = atoms // width
    full = per // 128
    spec = pl.BlockSpec((configs, parts, 2 * per), lambda i: (0, 0, i))
    sizes = (parts * full + 2, parts * full + 1)
    return pl.pallas_call(
        pack_kernel,
        grid=(width // 2,),
        in_specs=[spec, spec],
        out_specs=[pl.BlockSpec((2, n, configs, 128), lambda i: (i, 0, 0, 0)) for n in sizes],
        out_shape=[jax.ShapeDtypeStruct((width, n, configs, 128), BF16) for n in sizes],
        scratch_shapes=[VMEM((2, 2 * full + 1, 8 * configs, 128), F32)],
        compiler_params=params(),
        cost_estimate=cost(0, 8 * displacements.size),
    )(displacements, forces)


def one_hots(index_ref, full):
    index = index_ref[...]
    rows = index.shape[0]
    lane = lax.broadcasted_iota(jnp.int32, (rows, 128), 1)

    def hot(cond):
        return jnp.where(cond, 1.0, 0.0).astype(BF16)

    wholes = [hot(index - 128 * t == lane) for t in range(full)]
    rest = index - 128 * full
    lower = hot(rest == lane)
    upper = hot((rest >= 0) & (rest + 64 == lane))
    return wholes, lower, upper


def picked(wholes, half_hot, tiles, half):
    total = lax.dot_general(half_hot, half, NT, preferred_element_type=F32)
    for hot, tile in zip(wholes, tiles):
        total = total + lax.dot_general(hot, tile, NT, preferred_element_type=F32)
    return total


def flat(ref, t):
    block = ref[:, t]
    return block.reshape(block.shape[0] * block.shape[1], 128)


def gather_kernel(index_ref, recv_ref, disp_ref, wt_ref, wdisp_ref):
    clusters, dof, _ = disp_ref.shape
    atoms = dof // 3
    full = (recv_ref.shape[1] - 2) // 3
    wholes, lower, upper = one_hots(index_ref, full)
    for a in range(3):
        half_hot = upper if a == 1 else lower
        half = flat(recv_ref, 3 * full + a // 2)
        tiles = [flat(recv_ref, a * full + t) for t in range(full)]
        got = picked(wholes, half_hot, tiles, half)
        for c in range(clusters):
            disp_ref[c, a * atoms : (a + 1) * atoms] = got[c * atoms : (c + 1) * atoms].astype(BF16)


def gather(index, recv, clusters, atoms):
    configs = recv.shape[0] * recv.shape[2]
    return pl.pallas_call(
        lambda i, r, o: gather_kernel(i, r, o, None, None),
        in_specs=whole(index, recv),
        out_specs=pl.BlockSpec(memory_space=VMEM),
        out_shape=jax.ShapeDtypeStruct((clusters, 3 * atoms, configs), BF16),
        compiler_params=params(),
        cost_estimate=cost(2 * recv.size * index.size, 4 * recv.size),
    )(index, recv)


def residual_kernel(index_ref, recv1_ref, recv2_ref, harm_ref, out_ref):
    clusters, dof, _ = out_ref.shape
    atoms = dof // 3
    full = (recv2_ref.shape[1] - 1) // 3
    wholes, lower, upper = one_hots(index_ref, full)
    for a in range(3):
        half_hot = lower if a == 0 else upper
        half = flat(recv1_ref, 3 * full + 1) if a == 2 else flat(recv2_ref, 3 * full)
        tiles = [flat(recv2_ref, a * full + t) for t in range(full)]
        got = picked(wholes, half_hot, tiles, half)
        for c in range(clusters):
            rows = pl.ds(a * atoms, atoms)
            out_ref[c, rows] = (got[c * atoms : (c + 1) * atoms] + harm_ref[c, rows]).astype(BF16)


def residual_of(index, recv1, recv2, harmonic):
    return pl.pallas_call(
        residual_kernel,
        in_specs=whole(index, recv1, recv2, harmonic),
        out_specs=pl.BlockSpec(memory_space=VMEM),
        out_shape=jax.ShapeDtypeStruct(harmonic.shape, BF16),
        compiler_params=params(),
        cost_estimate=cost(2 * recv2.size * index.size, 8 * recv2.size),
    )(index, recv1, recv2, harmonic)


def load_frame(refs, frame, sem):
    layer = refs[0].shape[0]
    copies = [
        pltpu.make_async_copy(ref, frame.at[pl.ds(i * layer, layer)], sem.at[i])
        for i, ref in enumerate(refs)
    ]
    for copy in copies:
        copy.start()
    for copy in copies:
        copy.wait()


def harmonic_kernel(near_ref, phi_ref, low_ref, own_ref, high_ref, out_ref, frame, sem):
    c = pl.program_id(0)

    @pl.when(c == 0)
    def _():
        load_frame((low_ref, own_ref, high_ref), frame, sem)

    total = jnp.zeros(out_ref.shape[1:], F32)
    for k in range(phi_ref.shape[1]):
        total = total + jnp.dot(phi_ref[0, k], frame[near_ref[c, k]], preferred_element_type=F32)
    out_ref[0] = total


def harmonic_of(near, phi, low, own, high):
    clusters, blocks, dof, _ = phi.shape
    configs = own.shape[2]
    raw = pl.BlockSpec(memory_space=pl.ANY)
    return pl.pallas_call(
        harmonic_kernel,
        grid_spec=pltpu.PrefetchScalarGridSpec(
            num_scalar_prefetch=1,
            grid=(clusters,),
            in_specs=[
                pl.BlockSpec((1, blocks, dof, dof), lambda c, near: (c, 0, 0, 0)),
                raw,
                raw,
                raw,
            ],
            out_specs=pl.BlockSpec((1, dof, configs), lambda c, near: (c, 0, 0)),
            scratch_shapes=[
                VMEM((3 * own.shape[0], dof, configs), BF16),
                pltpu.SemaphoreType.DMA((3,)),
            ],
        ),
        out_shape=jax.ShapeDtypeStruct((clusters, dof, configs), F32),
        compiler_params=params(),
        cost_estimate=cost(2 * phi.size * configs, 2 * phi.size + 8 * own.size),
    )(near, phi, low, own, high)


def gradient_kernel(
    near_ref, wt_ref, dlow, down, dhigh, rlow, rown, rhigh, out_ref, disp, resid, sem
):
    c = pl.program_id(0)
    layer = pl.num_programs(0)

    @pl.when(c == 0)
    def _():
        load_frame((dlow, down, dhigh), disp, sem)
        load_frame((rlow, rown, rhigh), resid, sem)

    wt = wt_ref[...]
    wres = (resid[layer + c].astype(F32) * wt).astype(BF16)
    wdisp = (disp[layer + c].astype(F32) * wt).astype(BF16)
    for k in range(out_ref.shape[1]):
        n = near_ref[c, k]
        total = lax.dot_general(wres, disp[n], NT, preferred_element_type=F32)
        total = total + lax.dot_general(wdisp, resid[n], NT, preferred_element_type=F32)
        out_ref[0, k] = (0.5 * total).astype(BF16)


def gradient_of(near, wt, disp, resid):
    clusters, blocks = near.shape
    layer, dof, configs = disp[1].shape
    raw = pl.BlockSpec(memory_space=pl.ANY)
    return pl.pallas_call(
        gradient_kernel,
        grid_spec=pltpu.PrefetchScalarGridSpec(
            num_scalar_prefetch=1,
            grid=(clusters,),
            in_specs=[pl.BlockSpec((1, configs), lambda c, near: (0, 0))] + [raw] * 6,
            out_specs=pl.BlockSpec((1, blocks, dof, dof), lambda c, near: (c, 0, 0, 0)),
            scratch_shapes=[
                VMEM((3 * layer, dof, configs), BF16),
                VMEM((3 * layer, dof, configs), BF16),
                pltpu.SemaphoreType.DMA((3,)),
            ],
        ),
        out_shape=jax.ShapeDtypeStruct((clusters, blocks, dof, dof), BF16),
        compiler_params=params(),
        cost_estimate=cost(
            4 * clusters * blocks * dof * dof * configs, 2 * clusters * blocks * dof * dof
        ),
    )(near, wt, *disp, *resid)


def halo(block):
    count = lax.axis_size("cx")
    forward = [(i, (i + 1) % count) for i in range(count)]
    backward = [(b, a) for a, b in forward]
    return lax.ppermute(block, "cx", forward), lax.ppermute(block, "cx", backward)


def arrange(field, atom_map):
    picked_ = jnp.take(field, atom_map.reshape(-1), axis=2)
    picked_ = picked_.reshape(field.shape[0], 3, atom_map.shape[0], atom_map.shape[1])
    return jnp.transpose(picked_, (2, 1, 3, 0)).reshape(
        atom_map.shape[0], 3 * atom_map.shape[1], field.shape[0]
    )


def shards(displacements, forces, phi, neighbours, cluster_atoms, config_order, weights):
    width = lax.axis_size("cx")
    position = lax.axis_index("cx")
    layer, atoms = cluster_atoms.shape
    per = displacements.shape[2] // width
    offset = (neighbours // layer - position + 1 + width) % width
    near = offset * layer + neighbours % layer
    match = config_order[:, None] == jnp.arange(config_order.shape[0], dtype=jnp.int32)[None, :]
    wt = jnp.sum(jnp.where(match, weights[None, :], 0.0), axis=1)[None, :]
    atom_local = cluster_atoms - position * per
    dense = displacements.shape[0] % 16 == 0 and per % 128 == 64 and width % 2 == 0
    if dense:
        send1, send2 = pack(displacements, forces, width)
        recv1 = lax.all_to_all(send1, "cx", split_axis=0, concat_axis=0, tiled=True)
        recv2 = lax.all_to_all(send2, "cx", split_axis=0, concat_axis=0, tiled=True)
        index = ((atom_local - 64 * (position % 2) + per) % per).reshape(-1, 1)
        disp = gather(index, recv1, layer, atoms)
    else:
        disp, force = (
            arrange(
                lax.all_to_all(x, "cx", split_axis=2, concat_axis=0, tiled=True), atom_local
            )
            for x in (displacements, forces)
        )
    disp_low, disp_high = halo(disp)
    harmonic = harmonic_of(near, phi, disp_low, disp, disp_high)
    if dense:
        residual = residual_of(index, recv1, recv2, harmonic)
    else:
        residual = (force.astype(F32) + harmonic).astype(BF16)
    res_low, res_high = halo(residual)
    gradient = gradient_of(
        near, wt, (disp_low, disp, disp_high), (res_low, residual, res_high)
    )
    return residual, gradient


def solution(mesh):
    both = ("groups", "cx")
    in_specs = (
        P(both, None, None),
        P(both, None, None),
        P(both, None, None, None),
        P("cx", None),
        P("cx", None),
        P("groups"),
        P("groups"),
    )
    out_specs = (P(both, None, None), P(both, None, None, None))
    return jax.shard_map(shards, mesh=mesh, in_specs=in_specs, out_specs=out_specs, check_vma=False)
```

```python
import jax
import jax.numpy as jnp
from jax import lax
from jax.experimental import pallas as pl
from jax.experimental.pallas import tpu as pltpu
from jax.sharding import PartitionSpec as P

BF16 = jnp.bfloat16
F32 = jnp.float32
VMEM = pltpu.VMEM
SMEM = pltpu.SMEM
NT = (((1,), (1,)), ((), ()))
MIB = 1024 * 1024


def in_vmem(count):
    return [pl.BlockSpec(memory_space=VMEM)] * count


def in_smem():
    return pl.BlockSpec(memory_space=SMEM)


def in_place():
    return pl.BlockSpec(memory_space=pl.ANY)


def params(mib, **kw):
    return pltpu.CompilerParams(vmem_limit_bytes=mib * MIB, **kw)


def cost(flops, nbytes):
    return pl.CostEstimate(flops=flops, bytes_accessed=nbytes, transcendentals=0)


def shape(dims, dtype=BF16):
    return jax.ShapeDtypeStruct(dims, dtype)


def pack_kernel(disp_ref, force_ref, out1_ref, out2_ref):
    parts, configs, lanes = disp_ref.shape
    tiles = 2 * lanes // 128 // out1_ref.shape[0]
    full = tiles // 2
    low = lax.broadcasted_iota(jnp.int32, (configs, 128), 1) < 64
    for pair in range(out1_ref.shape[0] // 2):

        def tile(ref, a, t, pair=pair):
            return ref[a, :, pl.ds(128 * (pair * tiles + t), 128)]

        for e in range(2):
            first = e * (full + 1)

            def paired(ref0, a0, ref1, a1, e=e, tile=tile):
                x, y = tile(ref0, a0, full).astype(F32), tile(ref1, a1, full).astype(F32)
                if e == 0:
                    y = pltpu.roll(y, 64, 1)
                else:
                    x = pltpu.roll(x, 64, 1)
                return jnp.where(low, x, y).astype(BF16)

            dest = 2 * pair + e
            for a in range(parts):
                for t in range(full):
                    out1_ref[dest, a * full + t] = tile(disp_ref, a, first + t)
                    out2_ref[dest, a * full + t] = tile(force_ref, a, first + t)
            base = parts * full
            out1_ref[dest, base] = paired(disp_ref, 0, disp_ref, 1)
            out1_ref[dest, base + 1] = paired(disp_ref, 2, force_ref, 2)
            out2_ref[dest, base] = paired(force_ref, 0, force_ref, 1)


def pack(displacements, forces, width):
    parts, configs, atoms = displacements.shape
    per = atoms // width
    full = per // 128
    steps = 4 if width % 8 == 0 else width // 2
    group = width // steps
    spec = pl.BlockSpec((parts, configs, group * per), lambda i: (0, 0, i))
    sizes = (parts * full + 2, parts * full + 1)
    return pl.pallas_call(
        pack_kernel,
        grid=(steps,),
        in_specs=[spec, spec],
        out_specs=[pl.BlockSpec((group, n, configs, 128), lambda i: (i, 0, 0, 0)) for n in sizes],
        out_shape=[shape((width, n, configs, 128)) for n in sizes],
        compiler_params=params(8),
        cost_estimate=cost(0, 8 * displacements.size),
    )(displacements, forces)


def one_hots(index_ref, full):
    index = index_ref[...]
    rows = index.shape[0]
    lane = lax.broadcasted_iota(jnp.int32, (rows, 128), 1)

    def hot(cond):
        return jnp.where(cond, 1.0, 0.0).astype(BF16)

    wholes = [hot(index - 128 * t == lane) for t in range(full)]
    rest = index - 128 * full
    lower = hot(rest == lane)
    upper = hot((rest >= 0) & (rest + 64 == lane))
    return wholes, lower, upper


def picked(wholes, half_hot, tiles, half):
    total = lax.dot_general(half_hot, half, NT, preferred_element_type=F32)
    for hot, tile in zip(wholes, tiles):
        total = total + lax.dot_general(hot, tile, NT, preferred_element_type=F32)
    return total


def flat(ref, t):
    block = ref[:, t]
    return block.reshape(block.shape[0] * block.shape[1], 128)


def gather_kernel(index_ref, recv_ref, disp_ref):
    clusters, dof, _ = disp_ref.shape
    atoms = dof // 3
    full = (recv_ref.shape[1] - 2) // 3
    wholes, lower, upper = one_hots(index_ref, full)
    for a in range(3):
        half_hot = upper if a == 1 else lower
        half = flat(recv_ref, 3 * full + a // 2)
        tiles = [flat(recv_ref, a * full + t) for t in range(full)]
        got = picked(wholes, half_hot, tiles, half)
        for c in range(clusters):
            disp_ref[c, a * atoms : (a + 1) * atoms] = got[c * atoms : (c + 1) * atoms].astype(BF16)


def gather(index, recv, clusters, atoms):
    configs = recv.shape[0] * recv.shape[2]
    return pl.pallas_call(
        gather_kernel,
        in_specs=in_vmem(2),
        out_specs=in_vmem(1)[0],
        out_shape=shape((clusters, 3 * atoms, configs)),
        compiler_params=params(8),
        cost_estimate=cost(2 * recv.size * index.size, 4 * recv.size),
    )(index, recv)


def add_force_kernel(index_ref, recv1_ref, recv2_ref, harm_ref, out_ref):
    clusters, dof, _ = out_ref.shape
    atoms = dof // 3
    full = (recv2_ref.shape[1] - 1) // 3
    wholes, lower, upper = one_hots(index_ref, full)
    for a in range(3):
        half_hot = lower if a == 0 else upper
        half = flat(recv1_ref, 3 * full + 1) if a == 2 else flat(recv2_ref, 3 * full)
        tiles = [flat(recv2_ref, a * full + t) for t in range(full)]
        got = picked(wholes, half_hot, tiles, half)
        for c in range(clusters):
            rows = pl.ds(a * atoms, atoms)
            out_ref[c, rows] = got[c * atoms : (c + 1) * atoms] + harm_ref[c, rows]


def add_force(index, recv1, recv2, harmonic):
    return pl.pallas_call(
        add_force_kernel,
        in_specs=in_vmem(4),
        out_specs=in_vmem(1)[0],
        out_shape=shape(harmonic.shape, F32),
        compiler_params=params(8),
        cost_estimate=cost(2 * recv2.size * index.size, 8 * recv2.size),
    )(index, recv1, recv2, harmonic)


def blocks_for(block_ref, phi_ref, n):
    clusters, blocks = phi_ref.shape[:2]
    rows = []
    for c in range(clusters):
        k = block_ref[c, n]
        block = phi_ref[c, jnp.minimum(k, blocks - 1)]
        rows.append(jnp.where(k < blocks, block, jnp.zeros_like(block)))
    return jnp.concatenate(rows, axis=0)


def near_harmonic_kernel(block_ref, phi_ref, own_ref, partner_ref, out_ref):
    clusters, dof, configs = out_ref.shape
    layer = own_ref.shape[0]
    for n in range(2 * layer):
        disp = own_ref[n] if n < layer else partner_ref[n - layer]
        got = jnp.dot(blocks_for(block_ref, phi_ref, n), disp, preferred_element_type=F32)
        got = got.reshape(out_ref.shape)
        out_ref[...] = got if n == 0 else out_ref[...] + got


def near_harmonic(block_of, phi, own, partner):
    clusters, blocks, dof, _ = phi.shape
    configs = own.shape[2]
    return pl.pallas_call(
        near_harmonic_kernel,
        in_specs=[in_smem()] + in_vmem(3),
        out_specs=in_vmem(1)[0],
        out_shape=shape((clusters, dof, configs), F32),
        compiler_params=params(12),
        cost_estimate=cost(4 * phi.size * configs // 3, 4 * phi.size // 3),
    )(block_of, phi, own, partner)


def residual_kernel(
    block_ref, phi_ref, far_ref, base_ref, own_ref, wt_ref, out_ref, res_ref, left_ref, total
):
    clusters, dof, configs = out_ref.shape
    layer = far_ref.shape[0]
    for n in range(layer):
        left = blocks_for(block_ref, phi_ref, 2 * layer + n)
        got = jnp.dot(left, far_ref[n], preferred_element_type=F32).reshape(out_ref.shape)
        total[...] = (base_ref[...] if n == 0 else total[...]) + got
    wt = 0.5 * wt_ref[...]
    for c in range(clusters):
        res = total[c].astype(BF16)
        out_ref[c] = res
        res_ref[c] = res
        left_ref[c, :, :configs] = (res.astype(F32) * wt).astype(BF16)
        left_ref[c, :, configs:] = (own_ref[c].astype(F32) * wt).astype(BF16)


def residual_of(block_of, phi, far, base, own, wt):
    clusters, blocks, dof, _ = phi.shape
    configs = own.shape[2]
    return pl.pallas_call(
        residual_kernel,
        in_specs=[in_smem()] + in_vmem(5),
        out_specs=in_vmem(3),
        out_shape=[
            shape((clusters, dof, configs)),
            shape((clusters, dof, configs)),
            shape((clusters, dof, 2 * configs)),
        ],
        scratch_shapes=[VMEM((clusters, dof, configs), F32)],
        compiler_params=params(12),
        cost_estimate=cost(2 * phi.size * configs // 3, 2 * phi.size // 3),
    )(block_of, phi, far, base, own, wt)


def gradient_part(block_ref, left_ref, pairs, out_ref, held, sem, first):
    clusters, blocks, dof, _ = out_ref.shape
    width = left_ref.shape[2]
    left = left_ref[...].reshape(clusters * dof, width)

    def placed(i, c):
        k = block_ref[c, first + i]
        copy = pltpu.make_async_copy(
            held.at[i, c], out_ref.at[c, jnp.minimum(k, blocks - 1)], sem.at[i, c]
        )
        return k < blocks, copy

    for i, (disp_ref, res_ref, n) in enumerate(pairs):
        right = jnp.concatenate([disp_ref[n], res_ref[n]], axis=1)
        got = lax.dot_general(left, right, NT, preferred_element_type=F32)
        held[i] = got.astype(BF16).reshape(held.shape[1:])
        for c in range(clusters):
            there, copy = placed(i, c)
            pl.when(there)(copy.start)
    for i in range(len(pairs)):
        for c in range(clusters):
            there, copy = placed(i, c)
            pl.when(there)(copy.wait)


def near_gradient_kernel(block_ref, left_ref, down, dpart, rown, rpart, out_ref, held, sem):
    layer = down.shape[0]
    pairs = [(down, rown, n) for n in range(layer)] + [(dpart, rpart, n) for n in range(layer)]
    gradient_part(block_ref, left_ref, pairs, out_ref, held, sem, 0)


def far_gradient_kernel(block_ref, left_ref, dfar, rfar, prior_ref, out_ref, held, sem):
    layer = dfar.shape[0]
    pairs = [(dfar, rfar, n) for n in range(layer)]
    gradient_part(block_ref, left_ref, pairs, out_ref, held, sem, 2 * layer)


def gradient_call(kernel, layers, block_of, left, fields, out, prior):
    clusters, blocks, dof, _ = out.shape
    layer = fields[0].shape[0]
    count = layers * layer
    return pl.pallas_call(
        kernel,
        in_specs=[in_smem()] + in_vmem(1 + len(fields)) + [in_place()] * len(prior),
        out_specs=in_place(),
        out_shape=out,
        scratch_shapes=[
            VMEM((count, clusters, dof, dof), BF16),
            pltpu.SemaphoreType.DMA((count, clusters)),
        ],
        input_output_aliases={2 + len(fields): 0} if prior else {},
        compiler_params=params(8 * layers + 4),
        cost_estimate=cost(
            2 * count * dof * left.size, 2 * count * clusters * dof * dof
        ),
    )(block_of, left, *fields, *prior)


def swap_near(block):
    count = lax.axis_size("cx")
    return lax.ppermute(block, "cx", [(i, i ^ 1) for i in range(count)])


def swap_far(block):
    count = lax.axis_size("cx")
    pairs = [(i, (i + 1) % count if i % 2 else (i - 1) % count) for i in range(count)]
    return lax.ppermute(block, "cx", pairs)


def arrange(field, atom_map):
    taken = jnp.take(field, atom_map.reshape(-1), axis=2)
    taken = taken.reshape(field.shape[0], 3, atom_map.shape[0], atom_map.shape[1])
    return jnp.transpose(taken, (2, 1, 3, 0)).reshape(
        atom_map.shape[0], 3 * atom_map.shape[1], field.shape[0]
    )


def shards(displacements, forces, phi, neighbours, cluster_atoms, config_order, weights):
    width = lax.axis_size("cx")
    position = lax.axis_index("cx")
    layer, atoms = cluster_atoms.shape
    blocks = neighbours.shape[1]
    per = displacements.shape[2] // width
    offset = (neighbours // layer - position + 1 + width) % width
    partner = jnp.where(position % 2 == 0, 2, 0)
    group = jnp.where(offset == 1, 0, jnp.where(offset == partner, 1, 2))
    slot = group * layer + neighbours % layer
    named = slot[:, None, :] == jnp.arange(3 * layer, dtype=jnp.int32)[None, :, None]
    block_of = jnp.min(
        jnp.where(named, jnp.arange(blocks, dtype=jnp.int32)[None, None, :], blocks), axis=2
    )
    match = config_order[:, None] == jnp.arange(config_order.shape[0], dtype=jnp.int32)[None, :]
    wt = jnp.sum(jnp.where(match, weights[None, :], 0.0), axis=1)[None, :]
    atom_local = cluster_atoms - position * per
    dense = displacements.shape[0] % 16 == 0 and per % 128 == 64 and width % 2 == 0
    if dense:
        send1, send2 = pack(
            jnp.transpose(displacements, (1, 0, 2)), jnp.transpose(forces, (1, 0, 2)), width
        )
        recv1 = lax.all_to_all(send1, "cx", split_axis=0, concat_axis=0, tiled=True)
        recv2 = lax.all_to_all(send2, "cx", split_axis=0, concat_axis=0, tiled=True)
        index = ((atom_local - 64 * (position % 2) + per) % per).reshape(-1, 1)
        disp = gather(index, recv1, layer, atoms)
    else:
        disp, force = (
            arrange(lax.all_to_all(x, "cx", split_axis=2, concat_axis=0, tiled=True), atom_local)
            for x in (displacements, forces)
        )
    disp_near, disp_far = swap_near(disp), swap_far(disp)
    harmonic = near_harmonic(block_of, phi, disp, disp_near)
    if dense:
        base = add_force(index, recv1, recv2, harmonic)
    else:
        base = force.astype(F32) + harmonic
    residual, res, left = residual_of(block_of, phi, disp_far, base, disp, wt)
    res_near, res_far = swap_near(res), swap_far(res)
    out = shape(phi.shape)
    gradient = gradient_call(
        near_gradient_kernel, 2, block_of, left, (disp, disp_near, res, res_near), out, ()
    )
    gradient = gradient_call(
        far_gradient_kernel, 1, block_of, left, (disp_far, res_far), out, (gradient,)
    )
    return residual, gradient


def solution(mesh):
    both = ("groups", "cx")
    in_specs = (
        P(both, None, None),
        P(both, None, None),
        P(both, None, None, None),
        P("cx", None),
        P("cx", None),
        P("groups"),
        P("groups"),
    )
    out_specs = (P(both, None, None), P(both, None, None, None))
    return jax.shard_map(shards, mesh=mesh, in_specs=in_specs, out_specs=out_specs, check_vma=False)
```

```python
import functools

import jax
import jax.numpy as jnp
from jax import lax
from jax.experimental import pallas as pl
from jax.experimental.pallas import tpu as pltpu
from jax.sharding import PartitionSpec as P


BF16 = jnp.bfloat16
F32 = jnp.float32
VMEM = pltpu.VMEM
SMEM = pltpu.SMEM
NT = (((1,), (1,)), ((), ()))
MIB = 1024 * 1024


def in_vmem(count):
    return [pl.BlockSpec(memory_space=VMEM)] * count


def in_smem():
    return pl.BlockSpec(memory_space=SMEM)


def params(mib, **kw):
    return pltpu.CompilerParams(vmem_limit_bytes=mib * MIB, **kw)


def cost(flops, nbytes):
    return pl.CostEstimate(flops=flops, bytes_accessed=nbytes, transcendentals=0)


def shape(dims, dtype=BF16):
    return jax.ShapeDtypeStruct(dims, dtype)


def pack_kernel(disp_ref, force_ref, out_ref):
    parts, configs, lanes = disp_ref.shape
    tiles = 2 * lanes // 128 // out_ref.shape[0]
    full = tiles // 2
    low = lax.broadcasted_iota(jnp.int32, (configs, 128), 1) < 64
    for pair in range(out_ref.shape[0] // 2):

        def tile(ref, a, t, pair=pair):
            return ref[a, :, pl.ds(128 * (pair * tiles + t), 128)]

        for e in range(2):
            first = e * (full + 1)

            def paired(ref0, a0, ref1, a1, e=e, tile=tile):
                x, y = tile(ref0, a0, full).astype(F32), tile(ref1, a1, full).astype(F32)
                if e == 0:
                    y = pltpu.roll(y, 64, 1)
                else:
                    x = pltpu.roll(x, 64, 1)
                return jnp.where(low, x, y).astype(BF16)

            dest = 2 * pair + e
            base = parts * full
            for a in range(parts):
                for t in range(full):
                    out_ref[dest, a * full + t] = tile(disp_ref, a, first + t)
                    out_ref[dest, base + 3 + a * full + t] = tile(force_ref, a, first + t)
            out_ref[dest, base] = paired(disp_ref, 0, disp_ref, 1)
            out_ref[dest, base + 1] = paired(disp_ref, 2, force_ref, 2)
            out_ref[dest, base + 2] = paired(force_ref, 0, force_ref, 1)


def pack(displacements, forces, width):
    parts, configs, atoms = displacements.shape
    per = atoms // width
    steps = 4 if width % 8 == 0 else width // 2
    group = width // steps
    spec = pl.BlockSpec((parts, configs, group * per), lambda i: (0, 0, i))
    tiles = 2 * parts * (per // 128) + 3
    return pl.pallas_call(
        pack_kernel,
        grid=(steps,),
        in_specs=[spec, spec],
        out_specs=pl.BlockSpec((group, tiles, configs, 128), lambda i: (i, 0, 0, 0)),
        out_shape=shape((width, tiles, configs, 128)),
        compiler_params=params(60),
        cost_estimate=cost(0, 8 * displacements.size),
    )(displacements, forces)


def one_hots(index_ref, full):
    index = index_ref[...]
    rows = index.shape[0]
    lane = lax.broadcasted_iota(jnp.int32, (rows, 128), 1)

    def hot(cond):
        return jnp.where(cond, 1.0, 0.0).astype(BF16)

    wholes = [hot(index - 128 * t == lane) for t in range(full)]
    rest = index - 128 * full
    lower = hot(rest == lane)
    upper = hot((rest >= 0) & (rest + 64 == lane))
    return wholes, lower, upper


def picked(wholes, half_hot, tiles, half):
    total = lax.dot_general(half_hot, half, NT, preferred_element_type=F32)
    for hot, tile in zip(wholes, tiles):
        total = total + lax.dot_general(hot, tile, NT, preferred_element_type=F32)
    return total


def flat(ref, t):
    block = ref[:, t]
    return block.reshape(block.shape[0] * block.shape[1], 128)


def component(recv_ref, hots, field, a):
    wholes, lower, upper = hots
    full = len(wholes)
    base = 3 * full
    half = base + 1 if a == 2 else base + 2 * field
    first = a * full + field * (base + 3)
    half_hot = upper if (a == 1 if field == 0 else a > 0) else lower
    tiles = [flat(recv_ref, first + t) for t in range(full)]
    return picked(wholes, half_hot, tiles, flat(recv_ref, half))


def gather_kernel(field, index_ref, recv_ref, out_ref):
    clusters, dof, _ = out_ref.shape
    atoms = dof // 3
    hots = one_hots(index_ref, (recv_ref.shape[1] - 3) // 6)
    for a in range(3):
        got = component(recv_ref, hots, field, a).astype(BF16)
        for c in range(clusters):
            out_ref[c, a * atoms : (a + 1) * atoms] = got[c * atoms : (c + 1) * atoms]


def gather(index, recv, field, clusters, atoms):
    configs = recv.shape[0] * recv.shape[2]
    return pl.pallas_call(
        functools.partial(gather_kernel, field),
        in_specs=in_vmem(2),
        out_specs=in_vmem(1)[0],
        out_shape=shape((clusters, 3 * atoms, configs)),
        compiler_params=params(8),
        cost_estimate=cost(recv.size * index.size, 3 * recv.size),
    )(index, recv)


def masked(block_ref, held, n, c, blocks):
    block = held[c]
    return jnp.where(block_ref[c, n] < blocks, block, jnp.zeros_like(block))


def near_harmonic_kernel(
    block_ref, phi_ref, own_ref, partner_ref, force_ref, out_ref, far_ref, held, sem
):
    clusters, blocks = phi_ref.shape[:2]
    layer = own_ref.shape[0]

    def fetch(n, c):
        k = jnp.minimum(block_ref[c, n], blocks - 1)
        return pltpu.make_async_copy(phi_ref.at[c, k], held.at[n, c], sem.at[n, c])

    for n in range(3 * layer):
        for c in range(clusters):
            fetch(n, c).start()
    for n in range(2 * layer):
        for c in range(clusters):
            fetch(n, c).wait()
        disp = own_ref[n] if n < layer else partner_ref[n - layer]
        left = jnp.concatenate(
            [masked(block_ref, held.at[n], n, c, blocks) for c in range(clusters)], axis=0
        )
        got = jnp.dot(left, disp, preferred_element_type=F32).reshape(out_ref.shape)
        out_ref[...] = (force_ref[...].astype(F32) if n == 0 else out_ref[...]) + got
    for n in range(2 * layer, 3 * layer):
        for c in range(clusters):
            fetch(n, c).wait()
    for c in range(clusters):
        row = [
            masked(block_ref, held.at[n], n, c, blocks) for n in range(2 * layer, 3 * layer)
        ]
        far_ref[c] = jnp.concatenate(row, axis=1)


def near_harmonic(block_of, phi, own, partner, force):
    clusters, _, dof, _ = phi.shape
    layer, _, configs = own.shape
    return pl.pallas_call(
        near_harmonic_kernel,
        in_specs=[in_smem(), pl.BlockSpec(memory_space=pltpu.HBM)] + in_vmem(3),
        out_specs=in_vmem(2),
        out_shape=[
            shape((clusters, dof, configs), F32),
            shape((clusters, dof, layer * dof)),
        ],
        scratch_shapes=[
            VMEM((3 * layer, clusters, dof, dof), BF16),
            pltpu.SemaphoreType.DMA((3 * layer, clusters)),
        ],
        compiler_params=params(16),
        cost_estimate=cost(4 * phi.size * configs // 3, 2 * phi.size),
    )(block_of, pltpu.with_memory_space_constraint(phi, pltpu.HBM), own, partner, force)


def residual_kernel(phi_ref, far_ref, base_ref, own_ref, wt_ref, out_ref, res_ref, left_ref):
    clusters, _, configs = out_ref.shape
    far = far_ref[...].reshape(phi_ref.shape[2], configs)
    wt = 0.5 * wt_ref[...]
    for c in range(clusters):
        total = base_ref[c] + jnp.dot(phi_ref[c], far, preferred_element_type=F32)
        res = total.astype(BF16)
        out_ref[c] = res
        res_ref[c] = res
        left_ref[c, :, :configs] = (res.astype(F32) * wt).astype(BF16)
        left_ref[c, :, configs:] = (own_ref[c].astype(F32) * wt).astype(BF16)


def residual_of(phi_far, far, base, own, wt):
    clusters, dof, configs = own.shape
    return pl.pallas_call(
        residual_kernel,
        in_specs=in_vmem(5),
        out_specs=in_vmem(3),
        out_shape=[
            shape((clusters, dof, configs)),
            shape((clusters, dof, configs)),
            shape((clusters, dof, 2 * configs)),
        ],
        compiler_params=params(8),
        cost_estimate=cost(2 * phi_far.size * configs, 2 * phi_far.size),
    )(phi_far, far, base, own, wt)


def put_blocks(block_ref, held, out_ref, sem, first):
    clusters, blocks = out_ref.shape[:2]

    def placed(i, c, act):
        k = block_ref[c, first + i]
        copy = pltpu.make_async_copy(
            held.at[i, c], out_ref.at[c, jnp.minimum(k, blocks - 1)], sem.at[i, c]
        )
        pl.when(k < blocks)(getattr(copy, act))

    def start(i):
        for c in range(clusters):
            placed(i, c, "start")

    def finish():
        for i in range(held.shape[0]):
            for c in range(clusters):
                placed(i, c, "wait")

    return start, finish


def near_gradient_kernel(
    block_ref, left_ref, down, dnear, dfar, rown, rnear, out_ref, far_ref, held, sem
):
    clusters, dof, width = left_ref.shape
    layer, _, configs = down.shape
    start, finish = put_blocks(block_ref, held, out_ref, sem, 0)
    left = left_ref[...].reshape(clusters * dof, width)
    for i in range(2 * layer):
        disp, res = (down, rown) if i < layer else (dnear, rnear)
        right = jnp.concatenate([disp[i % layer], res[i % layer]], axis=1)
        got = lax.dot_general(left, right, NT, preferred_element_type=F32)
        held[i] = got.astype(BF16).reshape(held.shape[1:])
        start(i)
    for i in range(layer):
        got = lax.dot_general(left[:, :configs], dfar[i], NT, preferred_element_type=F32)
        far_ref[i] = got.reshape(far_ref.shape[1:])
    finish()


def near_gradient(block_of, left, fields, out):
    clusters, _, dof, _ = out.shape
    layer = fields[0].shape[0]
    return pl.pallas_call(
        near_gradient_kernel,
        in_specs=[in_smem()] + in_vmem(6),
        out_specs=[pl.BlockSpec(memory_space=pltpu.HBM)] + in_vmem(1),
        out_shape=[out, shape((layer, clusters, dof, dof), F32)],
        scratch_shapes=[
            VMEM((2 * layer, clusters, dof, dof), BF16),
            pltpu.SemaphoreType.DMA((2 * layer, clusters)),
        ],
        compiler_params=params(16),
        cost_estimate=cost(5 * layer * dof * left.size, 4 * layer * clusters * dof * dof),
    )(block_of, left, *fields)


def far_gradient_kernel(block_ref, left_ref, rfar, far_ref, prior_ref, out_ref, held, sem):
    clusters, dof, width = left_ref.shape
    layer, _, configs = rfar.shape
    start, finish = put_blocks(block_ref, held, out_ref, sem, 2 * layer)
    left = left_ref[:, :, configs:].reshape(clusters * dof, width - configs)
    for i in range(layer):
        got = lax.dot_general(left, rfar[i], NT, preferred_element_type=F32)
        held[i] = (far_ref[i] + got.reshape(far_ref.shape[1:])).astype(BF16)
        start(i)
    finish()


def far_gradient(block_of, left, rfar, far, prior):
    clusters, _, dof, _ = prior.shape
    layer = rfar.shape[0]
    return pl.pallas_call(
        far_gradient_kernel,
        in_specs=[in_smem()] + in_vmem(3) + [pl.BlockSpec(memory_space=pltpu.HBM)],
        out_specs=pl.BlockSpec(memory_space=pltpu.HBM),
        out_shape=shape(prior.shape),
        scratch_shapes=[
            VMEM((layer, clusters, dof, dof), BF16),
            pltpu.SemaphoreType.DMA((layer, clusters)),
        ],
        input_output_aliases={4: 0},
        compiler_params=params(8),
        cost_estimate=cost(layer * dof * left.size, 6 * layer * clusters * dof * dof),
    )(block_of, left, rfar, far, prior)


def swap_near(block):
    count = lax.axis_size("cx")
    return lax.ppermute(block, "cx", [(i, i ^ 1) for i in range(count)])


def swap_far(block):
    count = lax.axis_size("cx")
    pairs = [(i, (i + 1) % count if i % 2 else (i - 1) % count) for i in range(count)]
    return lax.ppermute(block, "cx", pairs)


def arrange(field, atom_map):
    taken = jnp.take(field, atom_map.reshape(-1), axis=2)
    taken = taken.reshape(field.shape[0], 3, atom_map.shape[0], atom_map.shape[1])
    return jnp.transpose(taken, (2, 1, 3, 0)).reshape(
        atom_map.shape[0], 3 * atom_map.shape[1], field.shape[0]
    )


def tables(neighbours, config_order, weights, layer, position, width):
    blocks = neighbours.shape[1]
    offset = (neighbours // layer - position + 1 + width) % width
    partner = jnp.where(position % 2 == 0, 2, 0)
    group = jnp.where(offset == 1, 0, jnp.where(offset == partner, 1, 2))
    slot = group * layer + neighbours % layer
    named = slot[:, None, :] == jnp.arange(3 * layer, dtype=jnp.int32)[None, :, None]
    block_of = jnp.min(
        jnp.where(named, jnp.arange(blocks, dtype=jnp.int32)[None, None, :], blocks), axis=2
    )
    match = config_order[:, None] == jnp.arange(config_order.shape[0], dtype=jnp.int32)[None, :]
    wt = jnp.sum(jnp.where(match, weights[None, :], 0.0), axis=1)[None, :]
    return block_of, wt


def shards(displacements, forces, phi, neighbours, cluster_atoms, config_order, weights):
    width = lax.axis_size("cx")
    position = lax.axis_index("cx")
    layer, atoms = cluster_atoms.shape
    per = displacements.shape[2] // width
    block_of, wt = tables(neighbours, config_order, weights, layer, position, width)
    atom_local = cluster_atoms - position * per
    if displacements.shape[0] % 16 == 0 and per % 128 == 64 and width % 2 == 0:
        send = pack(
            jnp.transpose(displacements, (1, 0, 2)), jnp.transpose(forces, (1, 0, 2)), width
        )
        recv = lax.all_to_all(send, "cx", split_axis=0, concat_axis=0, tiled=True)
        index = ((atom_local - 64 * (position % 2) + per) % per).reshape(-1, 1)
        disp = gather(index, recv, 0, layer, atoms)
        force = gather(index, recv, 1, layer, atoms)
    else:
        disp, force = (
            arrange(lax.all_to_all(x, "cx", split_axis=2, concat_axis=0, tiled=True), atom_local)
            for x in (displacements, forces)
        )
    disp_near, disp_far = swap_near(disp), swap_far(disp)
    base, phi_far = near_harmonic(block_of, phi, disp, disp_near, force)
    residual, res, left = residual_of(phi_far, disp_far, base, disp, wt)
    res_near, res_far = swap_near(res), swap_far(res)
    gradient, far = near_gradient(
        block_of, left, (disp, disp_near, disp_far, res, res_near), shape(phi.shape)
    )
    return residual, far_gradient(block_of, left, res_far, far, gradient)


def solution(mesh):
    both = ("groups", "cx")
    in_specs = (
        P(both, None, None),
        P(both, None, None),
        P(both, None, None, None),
        P("cx", None),
        P("cx", None),
        P("groups"),
        P("groups"),
    )
    out_specs = (P(both, None, None), P(both, None, None, None))
    return jax.shard_map(shards, mesh=mesh, in_specs=in_specs, out_specs=out_specs, check_vma=False)
```

```python
import functools

import jax
import jax.numpy as jnp
from jax import lax
from jax.experimental import pallas as pl
from jax.experimental.pallas import tpu as pltpu
from jax.sharding import PartitionSpec as P


BF16 = jnp.bfloat16
F32 = jnp.float32
VMEM = pltpu.VMEM
SMEM = pltpu.SMEM
NT = (((1,), (1,)), ((), ()))
MIB = 1024 * 1024


def in_vmem(count):
    return [pl.BlockSpec(memory_space=VMEM)] * count


def in_smem():
    return pl.BlockSpec(memory_space=SMEM)


def params(mib, **kw):
    return pltpu.CompilerParams(vmem_limit_bytes=mib * MIB, **kw)


def cost(flops, nbytes):
    return pl.CostEstimate(flops=flops, bytes_accessed=nbytes, transcendentals=0)


def shape(dims, dtype=BF16):
    return jax.ShapeDtypeStruct(dims, dtype)


def pack_kernel(disp_hbm, force_hbm, out_hbm, disp_ref, force_ref, out_ref, sem, out_sem):
    parts, configs, lanes = disp_ref.shape
    steps = sem.shape[1]
    group = out_ref.shape[0] // steps
    chunk = lanes // steps
    per_pair = 2 * lanes // out_ref.shape[0]
    full = per_pair // 256
    base = parts * full
    low = lax.broadcasted_iota(jnp.int32, (configs, 128), 1) < 64

    def fetch(field, i):
        source, target = ((disp_hbm, disp_ref), (force_hbm, force_ref))[field]
        cols = pl.ds(i * chunk, chunk)
        return pltpu.make_async_copy(
            source.at[:, :, cols], target.at[:, :, cols], sem.at[field, i]
        )

    def send(i):
        dests = pl.ds(i * group, group)
        return pltpu.make_async_copy(out_ref.at[dests], out_hbm.at[dests], out_sem.at[i])

    def tile(ref, a, pair, t):
        return ref[a, :, pl.ds(per_pair * pair + 128 * t, 128)]

    def paired(ref0, a0, ref1, a1, pair, e):
        x, y = tile(ref0, a0, pair, full).astype(F32), tile(ref1, a1, pair, full).astype(F32)
        if e == 0:
            y = pltpu.roll(y, 64, 1)
        else:
            x = pltpu.roll(x, 64, 1)
        return jnp.where(low, x, y).astype(BF16)

    for i in range(steps):
        for field in range(2):
            fetch(field, i).start()
    for i in range(steps):
        for field in range(2):
            fetch(field, i).wait()
        for dest in range(i * group, (i + 1) * group):
            pair, e = dest // 2, dest % 2
            first = e * (full + 1)
            for a in range(parts):
                for t in range(full):
                    out_ref[dest, a * full + t] = tile(disp_ref, a, pair, first + t)
                    out_ref[dest, base + 3 + a * full + t] = tile(force_ref, a, pair, first + t)
            out_ref[dest, base] = paired(disp_ref, 0, disp_ref, 1, pair, e)
            out_ref[dest, base + 1] = paired(disp_ref, 2, force_ref, 2, pair, e)
            out_ref[dest, base + 2] = paired(force_ref, 0, force_ref, 1, pair, e)
        send(i).start()
    for i in range(steps):
        send(i).wait()


def pack(displacements, forces, width):
    parts, configs, atoms = displacements.shape
    per = atoms // width
    steps = 4 if width % 8 == 0 else 1
    tiles = 2 * parts * (per // 128) + 3
    hbm = pl.BlockSpec(memory_space=pltpu.HBM)
    return pl.pallas_call(
        pack_kernel,
        in_specs=[hbm, hbm],
        out_specs=hbm,
        out_shape=shape((width, tiles, configs, 128)),
        scratch_shapes=[VMEM(displacements.shape, BF16)] * 2
        + [VMEM((width, tiles, configs, 128), BF16)]
        + [pltpu.SemaphoreType.DMA((2, steps)), pltpu.SemaphoreType.DMA((steps,))],
        compiler_params=params(8),
        cost_estimate=cost(0, 8 * displacements.size),
    )(*(pltpu.with_memory_space_constraint(x, pltpu.HBM) for x in (displacements, forces)))


def one_hots(index_ref, full):
    index = index_ref[...]
    rows = index.shape[0]
    lane = lax.broadcasted_iota(jnp.int32, (rows, 128), 1)

    def hot(cond):
        return jnp.where(cond, 1.0, 0.0).astype(BF16)

    wholes = [hot(index - 128 * t == lane) for t in range(full)]
    rest = index - 128 * full
    lower = hot(rest == lane)
    upper = hot((rest >= 0) & (rest + 64 == lane))
    return wholes, lower, upper


def picked(wholes, half_hot, tiles, half):
    total = lax.dot_general(half_hot, half, NT, preferred_element_type=F32)
    for hot, tile in zip(wholes, tiles):
        total = total + lax.dot_general(hot, tile, NT, preferred_element_type=F32)
    return total


def flat(ref, t):
    block = ref[:, t]
    return block.reshape(block.shape[0] * block.shape[1], 128)


def component(recv_ref, hots, field, a):
    wholes, lower, upper = hots
    full = len(wholes)
    base = 3 * full
    half = base + 1 if a == 2 else base + 2 * field
    first = a * full + field * (base + 3)
    half_hot = upper if (a == 1 if field == 0 else a > 0) else lower
    tiles = [flat(recv_ref, first + t) for t in range(full)]
    return picked(wholes, half_hot, tiles, flat(recv_ref, half))


def gather_kernel(field, index_ref, recv_ref, out_ref):
    clusters, dof, _ = out_ref.shape
    atoms = dof // 3
    hots = one_hots(index_ref, (recv_ref.shape[1] - 3) // 6)
    for a in range(3):
        got = component(recv_ref, hots, field, a).astype(BF16)
        for c in range(clusters):
            out_ref[c, a * atoms : (a + 1) * atoms] = got[c * atoms : (c + 1) * atoms]


def gather(index, recv, field, clusters, atoms):
    configs = recv.shape[0] * recv.shape[2]
    return pl.pallas_call(
        functools.partial(gather_kernel, field),
        in_specs=in_vmem(2),
        out_specs=in_vmem(1)[0],
        out_shape=shape((clusters, 3 * atoms, configs)),
        compiler_params=params(8),
        cost_estimate=cost(recv.size * index.size, 3 * recv.size),
    )(index, recv)


def order_kernel(block_ref, phi_ref, near_ref, far_ref):
    c = pl.program_id(0)
    blocks, dof = phi_ref.shape[1:3]
    near = near_ref.shape[2] // dof

    def block(n):
        k = block_ref[c, n]
        got = phi_ref[0, jnp.minimum(k, blocks - 1)]
        return jnp.where(k < blocks, got, jnp.zeros_like(got))

    near_ref[0] = jnp.concatenate([block(n) for n in range(near)], axis=1)
    far_ref[0] = jnp.concatenate([block(near + n) for n in range(near // 2)], axis=1)


def ordered(block_of, phi):
    clusters, blocks, dof, _ = phi.shape
    layer = block_of.shape[1] // 3
    widths = (2 * layer * dof, layer * dof)
    return pl.pallas_call(
        order_kernel,
        grid_spec=pltpu.PrefetchScalarGridSpec(
            num_scalar_prefetch=1,
            grid=(clusters,),
            in_specs=[pl.BlockSpec((1, blocks, dof, dof), lambda c, block: (c, 0, 0, 0))],
            out_specs=[pl.BlockSpec((1, dof, w), lambda c, block: (c, 0, 0)) for w in widths],
        ),
        out_shape=[shape((clusters, dof, w)) for w in widths],
        compiler_params=params(40),
        cost_estimate=cost(0, 4 * phi.size),
    )(block_of, phi)


def near_harmonic_kernel(phi_ref, own_ref, partner_ref, force_ref, wt_ref, out_ref, wdisp_ref):
    c = pl.program_id(0)
    depth = phi_ref.shape[2] // 2
    configs = own_ref.shape[2]
    total = force_ref[0].astype(F32)
    for i, ref in enumerate((own_ref, partner_ref)):
        left = phi_ref[0, :, depth * i : depth * (i + 1)]
        total = total + jnp.dot(
            left, ref[...].reshape(depth, configs), preferred_element_type=F32
        )
    out_ref[0] = total
    wdisp_ref[0] = (own_ref[c].astype(F32) * (0.5 * wt_ref[...])).astype(BF16)


def near_harmonic(phi_near, own, partner, force, wt):
    clusters, dof, width = phi_near.shape
    configs = own.shape[2]
    one = pl.BlockSpec((1, dof, configs), lambda c: (c, 0, 0))
    return pl.pallas_call(
        near_harmonic_kernel,
        grid=(clusters,),
        in_specs=[pl.BlockSpec((1, dof, width), lambda c: (c, 0, 0))]
        + in_vmem(2)
        + [one, pl.BlockSpec((1, configs), lambda c: (0, 0))],
        out_specs=[one, one],
        out_shape=[shape(own.shape, F32), shape(own.shape)],
        compiler_params=params(16),
        cost_estimate=cost(2 * phi_near.size * configs, 2 * phi_near.size),
    )(phi_near, own, partner, force, wt)


def residual_kernel(phi_ref, far_ref, base_ref, wt_ref, res_ref, wres_ref):
    clusters, _, configs = res_ref.shape
    far = far_ref[...].reshape(phi_ref.shape[2], configs)
    wt = 0.5 * wt_ref[...]
    for c in range(clusters):
        total = base_ref[c] + jnp.dot(phi_ref[c], far, preferred_element_type=F32)
        res = total.astype(BF16)
        res_ref[c] = res
        wres_ref[c] = (res.astype(F32) * wt).astype(BF16)


def residual_of(phi_far, far, base, wt):
    return pl.pallas_call(
        residual_kernel,
        in_specs=in_vmem(4),
        out_specs=in_vmem(2),
        out_shape=[shape(far.shape)] * 2,
        compiler_params=params(8),
        cost_estimate=cost(2 * phi_far.size * far.shape[2], 2 * phi_far.size),
    )(phi_far, far, base, wt)


def put_blocks(block_ref, held, out_ref, sem, first):
    clusters, blocks = out_ref.shape[:2]

    def placed(i, c, act):
        k = block_ref[c, first + i]
        copy = pltpu.make_async_copy(
            held.at[i, c], out_ref.at[c, jnp.minimum(k, blocks - 1)], sem.at[i, c]
        )
        pl.when(k < blocks)(getattr(copy, act))

    def start(i):
        for c in range(clusters):
            placed(i, c, "start")

    def finish():
        for i in range(held.shape[0]):
            for c in range(clusters):
                placed(i, c, "wait")

    return start, finish


def near_gradient_kernel(
    block_ref, wres_ref, wdisp_ref, down, dnear, dfar, rown, rnear, out_ref, whole_ref, far_ref,
    held, sem, whole_sem
):
    clusters, dof, configs = wres_ref.shape
    layer = down.shape[0]
    keep = pltpu.make_async_copy(rown, whole_ref, whole_sem)
    keep.start()
    start, finish = put_blocks(block_ref, held, out_ref, sem, 0)
    wres = wres_ref[...].reshape(clusters * dof, configs)
    wdisp = wdisp_ref[...].reshape(clusters * dof, configs)
    left = jnp.concatenate([wres, wdisp], axis=1)
    for i in range(2 * layer):
        disp, res = (down, rown) if i < layer else (dnear, rnear)
        right = jnp.concatenate([disp[i % layer], res[i % layer]], axis=1)
        got = lax.dot_general(left, right, NT, preferred_element_type=F32)
        held[i] = got.astype(BF16).reshape(held.shape[1:])
        start(i)
    for i in range(layer):
        got = lax.dot_general(wres, dfar[i], NT, preferred_element_type=F32)
        far_ref[i] = got.reshape(far_ref.shape[1:])
    finish()
    keep.wait()


def far_gradient_kernel(block_ref, wdisp_ref, rfar, far_ref, prior_ref, out_ref, held, sem):
    clusters, dof, configs = wdisp_ref.shape
    start, finish = put_blocks(block_ref, held, out_ref, sem, 2 * far_ref.shape[0])
    left = wdisp_ref[...].reshape(clusters * dof, configs)
    for i in range(rfar.shape[0]):
        got = lax.dot_general(left, rfar[i], NT, preferred_element_type=F32)
        held[i] = (far_ref[i] + got.reshape(held.shape[1:])).astype(BF16)
        start(i)
    finish()


def block_copies(count, clusters, dof):
    return [
        VMEM((count, clusters, dof, dof), BF16),
        pltpu.SemaphoreType.DMA((count, clusters)),
    ]


def near_gradient(block_of, wres, wdisp, fields, out):
    clusters, _, dof, _ = out.shape
    layer = fields[0].shape[0]
    hbm = pl.BlockSpec(memory_space=pltpu.HBM)
    return pl.pallas_call(
        near_gradient_kernel,
        in_specs=[in_smem()] + in_vmem(7),
        out_specs=[hbm, hbm] + in_vmem(1),
        out_shape=[out, shape(wres.shape), shape((layer, clusters, dof, dof), F32)],
        scratch_shapes=block_copies(2 * layer, clusters, dof) + [pltpu.SemaphoreType.DMA(())],
        compiler_params=params(16),
        cost_estimate=cost(10 * layer * dof * wres.size, 4 * layer * clusters * dof * dof),
    )(block_of, wres, wdisp, *fields)


def far_gradient(block_of, wdisp, rfar, far, prior):
    clusters, _, dof, _ = prior.shape
    layer = rfar.shape[0]
    hbm = pl.BlockSpec(memory_space=pltpu.HBM)
    return pl.pallas_call(
        far_gradient_kernel,
        in_specs=[in_smem()] + in_vmem(3) + [hbm],
        out_specs=hbm,
        out_shape=shape(prior.shape),
        scratch_shapes=block_copies(layer, clusters, dof),
        input_output_aliases={4: 0},
        compiler_params=params(8),
        cost_estimate=cost(2 * layer * dof * wdisp.size, 6 * layer * clusters * dof * dof),
    )(block_of, wdisp, rfar, far, prior)


def swap_near(block):
    count = lax.axis_size("cx")
    return lax.ppermute(block, "cx", [(i, i ^ 1) for i in range(count)])


def swap_far(block):
    count = lax.axis_size("cx")
    pairs = [(i, (i + 1) % count if i % 2 else (i - 1) % count) for i in range(count)]
    return lax.ppermute(block, "cx", pairs)


def arrange(field, atom_map):
    taken = jnp.take(field, atom_map.reshape(-1), axis=2)
    taken = taken.reshape(field.shape[0], 3, atom_map.shape[0], atom_map.shape[1])
    return jnp.transpose(taken, (2, 1, 3, 0)).reshape(
        atom_map.shape[0], 3 * atom_map.shape[1], field.shape[0]
    )


def tables(neighbours, config_order, weights, layer, position, width):
    blocks = neighbours.shape[1]
    offset = (neighbours // layer - position + 1 + width) % width
    partner = jnp.where(position % 2 == 0, 2, 0)
    group = jnp.where(offset == 1, 0, jnp.where(offset == partner, 1, 2))
    slot = group * layer + neighbours % layer
    named = slot[:, None, :] == jnp.arange(3 * layer, dtype=jnp.int32)[None, :, None]
    block_of = jnp.min(
        jnp.where(named, jnp.arange(blocks, dtype=jnp.int32)[None, None, :], blocks), axis=2
    )
    match = config_order[:, None] == jnp.arange(config_order.shape[0], dtype=jnp.int32)[None, :]
    wt = jnp.sum(jnp.where(match, weights[None, :], 0.0), axis=1)[None, :]
    return block_of, wt


def shards(displacements, forces, phi, neighbours, cluster_atoms, config_order, weights):
    width = lax.axis_size("cx")
    position = lax.axis_index("cx")
    layer, atoms = cluster_atoms.shape
    per = displacements.shape[2] // width
    block_of, wt = tables(neighbours, config_order, weights, layer, position, width)
    atom_local = cluster_atoms - position * per
    if displacements.shape[0] % 16 == 0 and per % 128 == 64 and width % 2 == 0:
        send = pack(
            jnp.transpose(displacements, (1, 0, 2)), jnp.transpose(forces, (1, 0, 2)), width
        )
        recv = lax.all_to_all(send, "cx", split_axis=0, concat_axis=0, tiled=True)
        index = ((atom_local - 64 * (position % 2) + per) % per).reshape(-1, 1)
        disp = gather(index, recv, 0, layer, atoms)
        force = gather(index, recv, 1, layer, atoms)
    else:
        disp, force = (
            arrange(lax.all_to_all(x, "cx", split_axis=2, concat_axis=0, tiled=True), atom_local)
            for x in (displacements, forces)
        )
    phi_near, phi_far = ordered(block_of, phi)
    disp_far = swap_far(disp)
    disp_near = swap_near(disp)
    base, wdisp = near_harmonic(phi_near, disp, disp_near, force, wt)
    res, wres = residual_of(phi_far, disp_far, base, wt)
    res_far = swap_far(res)
    res_near = swap_near(res)
    gradient, residual, far = near_gradient(
        block_of, wres, wdisp, (disp, disp_near, disp_far, res, res_near), shape(phi.shape)
    )
    return residual, far_gradient(block_of, wdisp, res_far, far, gradient)


def solution(mesh):
    both = ("groups", "cx")
    in_specs = (
        P(both, None, None),
        P(both, None, None),
        P(both, None, None, None),
        P("cx", None),
        P("cx", None),
        P("groups"),
        P("groups"),
    )
    out_specs = (P(both, None, None), P(both, None, None, None))
    return jax.shard_map(shards, mesh=mesh, in_specs=in_specs, out_specs=out_specs, check_vma=False)
```

```python
import functools

import jax
import jax.numpy as jnp
from jax import lax
from jax.experimental import pallas as pl
from jax.experimental.pallas import tpu as pltpu
from jax.sharding import PartitionSpec as P


BF16 = jnp.bfloat16
F32 = jnp.float32
VMEM = pltpu.VMEM
SMEM = pltpu.SMEM
NT = (((1,), (1,)), ((), ()))
MIB = 1024 * 1024


def in_vmem(count):
    return [pl.BlockSpec(memory_space=VMEM)] * count


def in_smem():
    return pl.BlockSpec(memory_space=SMEM)


def params(mib, **kw):
    return pltpu.CompilerParams(vmem_limit_bytes=mib * MIB, **kw)


def cost(flops, nbytes):
    return pl.CostEstimate(flops=flops, bytes_accessed=nbytes, transcendentals=0)


def shape(dims, dtype=BF16):
    return jax.ShapeDtypeStruct(dims, dtype)


def pack_kernel(disp_hbm, force_hbm, out_hbm, disp_ref, force_ref, out_ref, sem, out_sem):
    parts, configs, lanes = disp_ref.shape
    steps = sem.shape[1]
    group = out_ref.shape[0] // steps
    chunk = lanes // steps
    per_pair = 2 * lanes // out_ref.shape[0]
    full = per_pair // 256
    base = parts * full
    low = lax.broadcasted_iota(jnp.int32, (configs, 128), 1) < 64

    def fetch(field, i):
        source, target = ((disp_hbm, disp_ref), (force_hbm, force_ref))[field]
        cols = pl.ds(i * chunk, chunk)
        return pltpu.make_async_copy(
            source.at[:, :, cols], target.at[:, :, cols], sem.at[field, i]
        )

    def send(i):
        dests = pl.ds(i * group, group)
        return pltpu.make_async_copy(out_ref.at[dests], out_hbm.at[dests], out_sem.at[i])

    def tile(ref, a, pair, t):
        return ref[a, :, pl.ds(per_pair * pair + 128 * t, 128)]

    def paired(ref0, a0, ref1, a1, pair, e):
        x, y = tile(ref0, a0, pair, full).astype(F32), tile(ref1, a1, pair, full).astype(F32)
        if e == 0:
            y = pltpu.roll(y, 64, 1)
        else:
            x = pltpu.roll(x, 64, 1)
        return jnp.where(low, x, y).astype(BF16)

    for i in range(steps):
        for field in range(2):
            fetch(field, i).start()
    for i in range(steps):
        for field in range(2):
            fetch(field, i).wait()
        for dest in range(i * group, (i + 1) * group):
            pair, e = dest // 2, dest % 2
            first = e * (full + 1)
            for a in range(parts):
                for t in range(full):
                    out_ref[dest, a * full + t] = tile(disp_ref, a, pair, first + t)
                    out_ref[dest, base + 3 + a * full + t] = tile(force_ref, a, pair, first + t)
            out_ref[dest, base] = paired(disp_ref, 0, disp_ref, 1, pair, e)
            out_ref[dest, base + 1] = paired(disp_ref, 2, force_ref, 2, pair, e)
            out_ref[dest, base + 2] = paired(force_ref, 0, force_ref, 1, pair, e)
        send(i).start()
    for i in range(steps):
        send(i).wait()


def pack(displacements, forces, width):
    parts, configs, atoms = displacements.shape
    per = atoms // width
    steps = 4 if width % 8 == 0 else 1
    tiles = 2 * parts * (per // 128) + 3
    hbm = pl.BlockSpec(memory_space=pltpu.HBM)
    return pl.pallas_call(
        pack_kernel,
        in_specs=[hbm, hbm],
        out_specs=hbm,
        out_shape=shape((width, tiles, configs, 128)),
        scratch_shapes=[VMEM(displacements.shape, BF16)] * 2
        + [VMEM((width, tiles, configs, 128), BF16)]
        + [pltpu.SemaphoreType.DMA((2, steps)), pltpu.SemaphoreType.DMA((steps,))],
        compiler_params=params(8),
        cost_estimate=cost(0, 8 * displacements.size),
    )(*(pltpu.with_memory_space_constraint(x, pltpu.HBM) for x in (displacements, forces)))


def one_hots(index_ref, full):
    index = index_ref[...]
    rows = index.shape[0]
    lane = lax.broadcasted_iota(jnp.int32, (rows, 128), 1)

    def hot(cond):
        return jnp.where(cond, 1.0, 0.0).astype(BF16)

    wholes = [hot(index - 128 * t == lane) for t in range(full)]
    rest = index - 128 * full
    lower = hot(rest == lane)
    upper = hot((rest >= 0) & (rest + 64 == lane))
    return wholes, lower, upper


def picked(wholes, half_hot, tiles, half):
    total = lax.dot_general(half_hot, half, NT, preferred_element_type=F32)
    for hot, tile in zip(wholes, tiles):
        total = total + lax.dot_general(hot, tile, NT, preferred_element_type=F32)
    return total


def flat(ref, t):
    block = ref[:, t]
    return block.reshape(block.shape[0] * block.shape[1], 128)


def component(recv_ref, hots, field, a):
    wholes, lower, upper = hots
    full = len(wholes)
    base = 3 * full
    half = base + 1 if a == 2 else base + 2 * field
    first = a * full + field * (base + 3)
    half_hot = upper if (a == 1 if field == 0 else a > 0) else lower
    tiles = [flat(recv_ref, first + t) for t in range(full)]
    return picked(wholes, half_hot, tiles, flat(recv_ref, half))


def put(out_ref, index_ref, recv_ref, field, dtype):
    clusters, dof, _ = out_ref.shape
    atoms = dof // 3
    hots = one_hots(index_ref, recv_ref.shape[1] // (6 if recv_ref.shape[1] % 3 == 0 else 3))
    for a in range(3):
        got = component(recv_ref, hots, field, a).astype(dtype)
        for c in range(clusters):
            out_ref[c, a * atoms : (a + 1) * atoms] = got[c * atoms : (c + 1) * atoms]


def gather_and_pass_kernel(route_ref, index_ref, recv_ref, out_ref, pass_ref):
    for i in range(pass_ref.shape[0]):
        pass_ref[i] = recv_ref[route_ref[3, i], : pass_ref.shape[1]]
    put(out_ref, index_ref, recv_ref, 0, BF16)


def disp_tiles(recv):
    return 3 * ((recv.shape[1] - 3) // 6) + 2


def gather_and_pass(route, index, recv, clusters, atoms):
    width, _, configs, _ = recv.shape
    return pl.pallas_call(
        gather_and_pass_kernel,
        in_specs=[in_smem()] + in_vmem(2),
        out_specs=in_vmem(2),
        out_shape=[
            shape((clusters, 3 * atoms, width * configs)),
            shape((route.shape[1], disp_tiles(recv), configs, 128)),
        ],
        compiler_params=params(8),
        cost_estimate=cost(recv.size * index.size, 3 * recv.size),
    )(route, index, recv)


def pick_kernel(route_ref, send_ref, *rest):
    outs, sem = rest[:-1], rest[-1]
    copies = [
        pltpu.make_async_copy(
            send_ref.at[route_ref[0, j], pl.ds(0, out.shape[0])], out, sem.at[j]
        )
        for j, out in enumerate(outs)
    ]
    for copy in copies:
        copy.start()
    for copy in copies:
        copy.wait()


def pick(route, send):
    reach = route.shape[1]
    _, _, configs, _ = send.shape
    return pl.pallas_call(
        pick_kernel,
        in_specs=[in_smem(), pl.BlockSpec(memory_space=pltpu.HBM)],
        out_specs=in_vmem(reach),
        out_shape=[shape((disp_tiles(send), configs, 128))] * reach,
        scratch_shapes=[pltpu.SemaphoreType.DMA((reach,))],
        compiler_params=params(60),
        cost_estimate=cost(0, send.size),
    )(route, pltpu.with_memory_space_constraint(send, pltpu.HBM))


def masked(block_ref, block, c, n, blocks):
    return jnp.where(block_ref[c, n] < blocks, block, jnp.zeros_like(block))


def order_kernel(block_ref, phi_ref, out_ref, held, sem):
    clusters, blocks = phi_ref.shape[:2]
    layer = held.shape[1]

    def fetch(c, n):
        k = jnp.minimum(block_ref[c, 2 * layer + n], blocks - 1)
        return pltpu.make_async_copy(phi_ref.at[c, k], held.at[c, n], sem.at[c, n])

    for c in range(clusters):
        for n in range(layer):
            fetch(c, n).start()
    for c in range(clusters):
        for n in range(layer):
            fetch(c, n).wait()
        row = [masked(block_ref, held[c, n], c, 2 * layer + n, blocks) for n in range(layer)]
        out_ref[c] = jnp.concatenate(row, axis=1)


def ordered(block_of, phi):
    clusters, _, dof, _ = phi.shape
    layer = block_of.shape[1] // 3
    return pl.pallas_call(
        order_kernel,
        in_specs=[in_smem(), pl.BlockSpec(memory_space=pltpu.HBM)],
        out_specs=in_vmem(1)[0],
        out_shape=shape((clusters, dof, layer * dof)),
        scratch_shapes=[
            VMEM((clusters, layer, dof, dof), BF16),
            pltpu.SemaphoreType.DMA((clusters, layer)),
        ],
        compiler_params=params(60),
        cost_estimate=cost(0, 2 * phi.size),
    )(block_of, pltpu.with_memory_space_constraint(phi, pltpu.HBM))


def stacked(block_ref, held, n, blocks):
    clusters = held.shape[0]
    return jnp.concatenate(
        [masked(block_ref, held[c], c, n, blocks) for c in range(clusters)], axis=0
    )


def fetcher(block_ref, phi_ref, sem):
    def fetch(n, c, place):
        k = jnp.minimum(block_ref[c, n], phi_ref.shape[1] - 1)
        return pltpu.make_async_copy(phi_ref.at[c, k], place.at[c], sem.at[n, c])

    return fetch


def own_harmonic(block_ref, blocks, own_ref, held, out_ref, ready):
    for n in range(own_ref.shape[0]):
        ready(n)
        left = stacked(block_ref, held.at[n], n, blocks)
        got = jnp.dot(left, own_ref[n], preferred_element_type=F32)
        out_ref[...] = out_ref[...] + got.reshape(out_ref.shape)


def own_kernel(block_ref, phi_ref, own_ref, wt_ref, *rest, dense):
    if dense:
        route_ref, index_ref, index_far_ref, recv_ref, *rest = rest
        reach = route_ref.shape[1]
        pieces, rest = rest[:reach], rest[reach:]
        out_ref, wdisp_ref, partner_ref, direct_ref, held, sem, frame, frame_sem = rest
        copies = [
            pltpu.make_async_copy(
                piece, frame.at[lax.rem(route_ref[1, j], reach)], frame_sem.at[j]
            )
            for j, piece in enumerate(pieces)
        ]
    else:
        force_ref, out_ref, wdisp_ref, partner_ref, held, sem = rest
        copies = []
    layer = own_ref.shape[0]
    clusters, blocks = phi_ref.shape[:2]
    fetch = fetcher(block_ref, phi_ref, sem)
    for n in range(2 * layer):
        for c in range(clusters):
            place = held.at[n] if n < layer else partner_ref.at[n - layer]
            fetch(n, c, place).start()
    for copy in copies:
        copy.start()
    wt = 0.5 * wt_ref[...]
    for c in range(clusters):
        wdisp_ref[c] = (own_ref[c].astype(F32) * wt).astype(BF16)
    if dense:
        put(out_ref, index_ref, recv_ref, 1, F32)
    else:
        out_ref[...] = force_ref[...].astype(F32)

    def ready(n):
        for c in range(clusters):
            fetch(n, c, held.at[n] if n < layer else partner_ref.at[n - layer]).wait()

    own_harmonic(block_ref, blocks, own_ref, held, out_ref, ready)
    for copy in copies:
        copy.wait()
    if dense:
        put(direct_ref, index_far_ref, frame, 0, BF16)
    for n in range(layer, 2 * layer):
        ready(n)


def own_part(block_of, phi, own, wt, dense, extra):
    clusters, _, dof, _ = phi.shape
    layer, _, configs = own.shape
    hbm = pl.BlockSpec(memory_space=pltpu.HBM)
    in_specs = [in_smem(), hbm] + in_vmem(2)
    out_shape = [shape(own.shape, F32), shape(own.shape), shape((layer, clusters, dof, dof))]
    scratch = [
        VMEM((layer, clusters, dof, dof), BF16),
        pltpu.SemaphoreType.DMA((2 * layer, clusters)),
    ]
    if dense:
        pieces = extra[4:]
        tiles, few, _ = pieces[0].shape
        in_specs += [in_smem()] + in_vmem(3) + [hbm] * len(pieces)
        out_shape.append(shape((clusters, dof, len(pieces) * few)))
        scratch += [
            VMEM((len(pieces), tiles, few, 128), BF16),
            pltpu.SemaphoreType.DMA((len(pieces),)),
        ]
        pieces = [pltpu.with_memory_space_constraint(p, pltpu.HBM) for p in pieces]
        extra = (*extra[:4], *pieces)
    else:
        in_specs += in_vmem(1)
    return pl.pallas_call(
        functools.partial(own_kernel, dense=dense),
        in_specs=in_specs,
        out_specs=in_vmem(len(out_shape)),
        out_shape=out_shape,
        scratch_shapes=scratch,
        compiler_params=params(12),
        cost_estimate=cost(phi.size * configs, 2 * phi.size),
    )(block_of, pltpu.with_memory_space_constraint(phi, pltpu.HBM), own, wt, *extra)


def partner_kernel(blocks, block_ref, phi_ref, partner_ref, base_ref, out_ref):
    layer = partner_ref.shape[0]
    for n in range(layer):
        left = stacked(block_ref, phi_ref.at[n], layer + n, blocks)
        got = jnp.dot(left, partner_ref[n], preferred_element_type=F32).reshape(out_ref.shape)
        out_ref[...] = (base_ref if n == 0 else out_ref)[...] + got


def partner_part(blocks, block_of, phi_partner, partner, base):
    return pl.pallas_call(
        functools.partial(partner_kernel, blocks),
        in_specs=[in_smem()] + in_vmem(3),
        out_specs=in_vmem(1)[0],
        out_shape=shape(base.shape, F32),
        compiler_params=params(8),
        cost_estimate=cost(2 * phi_partner.size * base.shape[2], 2 * phi_partner.size),
    )(block_of, phi_partner, partner, base)


def residual_kernel(phi_ref, far_ref, base_ref, wt_ref, res_ref, wres_ref):
    clusters, _, configs = res_ref.shape
    far = far_ref[...].reshape(phi_ref.shape[2], configs)
    wt = 0.5 * wt_ref[...]
    for c in range(clusters):
        total = base_ref[c] + jnp.dot(phi_ref[c], far, preferred_element_type=F32)
        res = total.astype(BF16)
        res_ref[c] = res
        wres_ref[c] = (res.astype(F32) * wt).astype(BF16)


def residual_of(phi_far, far, base, wt):
    return pl.pallas_call(
        residual_kernel,
        in_specs=in_vmem(4),
        out_specs=in_vmem(2),
        out_shape=[shape(far.shape)] * 2,
        compiler_params=params(8),
        cost_estimate=cost(2 * phi_far.size * far.shape[2], 2 * phi_far.size),
    )(phi_far, far, base, wt)


def merged_residual_kernel(
    route_ref, index_ref, recv_ref, direct_ref, phi_ref, base_ref, wt_ref, res_ref, wres_ref,
    far_ref
):
    clusters, dof, configs = res_ref.shape
    atoms = dof // 3
    half = configs // 2
    first = route_ref[1, 0] < route_ref.shape[1]
    hots = one_hots(index_ref, (recv_ref.shape[1] - 2) // 3)
    for a in range(3):
        rest = component(recv_ref, hots, 0, a).astype(BF16)
        for c in range(clusters):
            rows = pl.ds(a * atoms, atoms)
            x, y = direct_ref[c, rows], rest[c * atoms : (c + 1) * atoms]
            far_ref[c, rows, :half] = jnp.where(first, x, y)
            far_ref[c, rows, half:] = jnp.where(first, y, x)
    residual_kernel(phi_ref, far_ref, base_ref, wt_ref, res_ref, wres_ref)


def merged_residual(route, index, recv, near_half, phi_far, base, wt):
    return pl.pallas_call(
        merged_residual_kernel,
        in_specs=[in_smem()] + in_vmem(6),
        out_specs=in_vmem(3),
        out_shape=[shape(base.shape)] * 3,
        compiler_params=params(8),
        cost_estimate=cost(
            2 * phi_far.size * base.shape[2] + recv.size * index.size, 2 * phi_far.size
        ),
    )(route, index, recv, near_half, phi_far, base, wt)


def put_blocks(block_ref, held, out_ref, sem, first):
    clusters, blocks = out_ref.shape[:2]

    def placed(i, c, act):
        k = block_ref[c, first + i]
        copy = pltpu.make_async_copy(
            held.at[i, c], out_ref.at[c, jnp.minimum(k, blocks - 1)], sem.at[i, c]
        )
        pl.when(k < blocks)(getattr(copy, act))

    def start(i):
        for c in range(clusters):
            placed(i, c, "start")

    def finish():
        for i in range(held.shape[0]):
            for c in range(clusters):
                placed(i, c, "wait")

    return start, finish


def near_gradient_kernel(
    block_ref, wres_ref, wdisp_ref, down, dnear, dfar, rown, rnear, out_ref, whole_ref, far_ref,
    held, sem, whole_sem
):
    clusters, dof, configs = wres_ref.shape
    layer = down.shape[0]
    keep = pltpu.make_async_copy(rown, whole_ref, whole_sem)
    keep.start()
    start, finish = put_blocks(block_ref, held, out_ref, sem, 0)
    wres = wres_ref[...].reshape(clusters * dof, configs)
    wdisp = wdisp_ref[...].reshape(clusters * dof, configs)
    left = jnp.concatenate([wres, wdisp], axis=1)
    for i in range(2 * layer):
        disp, res = (down, rown) if i < layer else (dnear, rnear)
        right = jnp.concatenate([disp[i % layer], res[i % layer]], axis=1)
        got = lax.dot_general(left, right, NT, preferred_element_type=F32)
        held[i] = got.astype(BF16).reshape(held.shape[1:])
        start(i)
    for i in range(layer):
        got = lax.dot_general(wres, dfar[i], NT, preferred_element_type=F32)
        far_ref[i] = got.reshape(far_ref.shape[1:])
    finish()
    keep.wait()


def far_gradient_kernel(block_ref, wdisp_ref, rfar, far_ref, prior_ref, out_ref, held, sem):
    clusters, dof, configs = wdisp_ref.shape
    start, finish = put_blocks(block_ref, held, out_ref, sem, 2 * far_ref.shape[0])
    left = wdisp_ref[...].reshape(clusters * dof, configs)
    for i in range(rfar.shape[0]):
        got = lax.dot_general(left, rfar[i], NT, preferred_element_type=F32)
        held[i] = (far_ref[i] + got.reshape(held.shape[1:])).astype(BF16)
        start(i)
    finish()


def block_copies(count, clusters, dof):
    return [
        VMEM((count, clusters, dof, dof), BF16),
        pltpu.SemaphoreType.DMA((count, clusters)),
    ]


def near_gradient(block_of, wres, wdisp, fields, out):
    clusters, _, dof, _ = out.shape
    layer = fields[0].shape[0]
    hbm = pl.BlockSpec(memory_space=pltpu.HBM)
    return pl.pallas_call(
        near_gradient_kernel,
        in_specs=[in_smem()] + in_vmem(7),
        out_specs=[hbm, hbm] + in_vmem(1),
        out_shape=[out, shape(wres.shape), shape((layer, clusters, dof, dof), F32)],
        scratch_shapes=block_copies(2 * layer, clusters, dof) + [pltpu.SemaphoreType.DMA(())],
        compiler_params=params(16),
        cost_estimate=cost(10 * layer * dof * wres.size, 4 * layer * clusters * dof * dof),
    )(block_of, wres, wdisp, *fields)


def far_gradient(block_of, wdisp, rfar, far, prior):
    clusters, _, dof, _ = prior.shape
    layer = rfar.shape[0]
    hbm = pl.BlockSpec(memory_space=pltpu.HBM)
    return pl.pallas_call(
        far_gradient_kernel,
        in_specs=[in_smem()] + in_vmem(3) + [hbm],
        out_specs=hbm,
        out_shape=shape(prior.shape),
        scratch_shapes=block_copies(layer, clusters, dof),
        input_output_aliases={4: 0},
        compiler_params=params(8),
        cost_estimate=cost(2 * layer * dof * wdisp.size, 6 * layer * clusters * dof * dof),
    )(block_of, wdisp, rfar, far, prior)


def swap_near(block):
    count = lax.axis_size("cx")
    return lax.ppermute(block, "cx", [(i, i ^ 1) for i in range(count)])


def swap_far(block):
    count = lax.axis_size("cx")
    pairs = [(i, (i + 1) % count if i % 2 else (i - 1) % count) for i in range(count)]
    return lax.ppermute(block, "cx", pairs)


def far_of(i, count):
    return (i + 2 * (i % 2) - 1) % count


def routes(position, width, reach):
    q = jnp.arange(reach, dtype=jnp.int32)[None, :]
    row = jnp.arange(4, dtype=jnp.int32)[:, None]
    block = position // reach * reach
    far_block = far_of(position, width) // reach * reach
    peer = position ^ q
    rest = (jnp.where(row == 2, block, far_block) + reach + q) % width
    return jnp.where(row == 0, far_of(peer, width), jnp.where(row == 1, peer, rest))


def arrange(field, atom_map):
    taken = jnp.take(field, atom_map.reshape(-1), axis=2)
    taken = taken.reshape(field.shape[0], 3, atom_map.shape[0], atom_map.shape[1])
    return jnp.transpose(taken, (2, 1, 3, 0)).reshape(
        atom_map.shape[0], 3 * atom_map.shape[1], field.shape[0]
    )


def tables(neighbours, config_order, weights, layer, position, width):
    blocks = neighbours.shape[1]
    offset = (neighbours // layer - position + 1 + width) % width
    partner = jnp.where(position % 2 == 0, 2, 0)
    group = jnp.where(offset == 1, 0, jnp.where(offset == partner, 1, 2))
    slot = group * layer + neighbours % layer
    named = slot[:, None, :] == jnp.arange(3 * layer, dtype=jnp.int32)[None, :, None]
    block_of = jnp.min(
        jnp.where(named, jnp.arange(blocks, dtype=jnp.int32)[None, None, :], blocks), axis=2
    )
    match = config_order[:, None] == jnp.arange(config_order.shape[0], dtype=jnp.int32)[None, :]
    wt = jnp.sum(jnp.where(match, weights[None, :], 0.0), axis=1)[None, :]
    return block_of, wt


def shards(displacements, forces, phi, neighbours, cluster_atoms, config_order, weights):
    width = lax.axis_size("cx")
    position = lax.axis_index("cx")
    layer, atoms = cluster_atoms.shape
    per = displacements.shape[2] // width
    block_of, wt = tables(neighbours, config_order, weights, layer, position, width)
    atom_local = cluster_atoms - position * per
    reach = width // 2
    dense = displacements.shape[0] % 16 == 0 and per % 128 == 64
    dense = dense and reach & (reach - 1) == 0 and displacements.shape[0] * reach % 128 == 0
    phi_far = ordered(block_of, phi)
    if dense:
        send = pack(
            jnp.transpose(displacements, (1, 0, 2)), jnp.transpose(forces, (1, 0, 2)), width
        )
        recv = lax.all_to_all(send, "cx", split_axis=0, concat_axis=0, tiled=True)
        index = (atom_local - 64 * (position % 2) + per) % per
        route = routes(position, width, reach)
        index_far = swap_far(index).reshape(-1, 1)
        index = index.reshape(-1, 1)
        pieces = list(pick(route, send))
        for j in range(1, reach):
            pieces[j] = lax.ppermute(pieces[j], "cx", [(i, i ^ j) for i in range(width)])
        disp, passed = gather_and_pass(route, index, recv, layer, atoms)
        recv_far = swap_far(passed)
        extra = (route, index, index_far, recv, *pieces)
    else:
        disp, force = (
            arrange(lax.all_to_all(x, "cx", split_axis=2, concat_axis=0, tiled=True), atom_local)
            for x in (displacements, forces)
        )
        disp_far = swap_far(disp)
        extra = (force,)
    disp_near = swap_near(disp)
    base, wdisp, phi_partner, *near_half = own_part(block_of, phi, disp, wt, dense, extra)
    base = partner_part(phi.shape[1], block_of, phi_partner, disp_near, base)
    if dense:
        res, wres, disp_far = merged_residual(
            route, index_far, recv_far, near_half[0], phi_far, base, wt
        )
    else:
        res, wres = residual_of(phi_far, disp_far, base, wt)
    res_far = swap_far(res)
    res_near = swap_near(res)
    gradient, residual, far = near_gradient(
        block_of, wres, wdisp, (disp, disp_near, disp_far, res, res_near), shape(phi.shape)
    )
    return residual, far_gradient(block_of, wdisp, res_far, far, gradient)


def solution(mesh):
    both = ("groups", "cx")
    in_specs = (
        P(both, None, None),
        P(both, None, None),
        P(both, None, None, None),
        P("cx", None),
        P("cx", None),
        P("groups"),
        P("groups"),
    )
    out_specs = (P(both, None, None), P(both, None, None, None))
    return jax.shard_map(shards, mesh=mesh, in_specs=in_specs, out_specs=out_specs, check_vma=False)
```

```python
import functools

import jax
import jax.numpy as jnp
from jax import lax
from jax.experimental import pallas as pl
from jax.experimental.pallas import tpu as pltpu
from jax.sharding import PartitionSpec as P


BF16 = jnp.bfloat16
F32 = jnp.float32
VMEM = pltpu.VMEM
SMEM = pltpu.SMEM
NT = (((1,), (1,)), ((), ()))
MIB = 1024 * 1024


def in_vmem(count):
    return [pl.BlockSpec(memory_space=VMEM)] * count


def in_smem():
    return pl.BlockSpec(memory_space=SMEM)


def params(mib, **kw):
    return pltpu.CompilerParams(vmem_limit_bytes=mib * MIB, **kw)


def cost(flops, nbytes):
    return pl.CostEstimate(flops=flops, bytes_accessed=nbytes, transcendentals=0)


def shape(dims, dtype=BF16):
    return jax.ShapeDtypeStruct(dims, dtype)


def pack_kernel(disp_hbm, force_hbm, out_hbm, disp_ref, force_ref, out_ref, sem, out_sem):
    parts, configs, lanes = disp_ref.shape
    steps = sem.shape[1]
    group = out_ref.shape[0] // steps
    chunk = lanes // steps
    per_pair = 2 * lanes // out_ref.shape[0]
    full = per_pair // 256
    base = parts * full
    low = lax.broadcasted_iota(jnp.int32, (configs, 128), 1) < 64

    def fetch(field, i):
        source, target = ((disp_hbm, disp_ref), (force_hbm, force_ref))[field]
        cols = pl.ds(i * chunk, chunk)
        return pltpu.make_async_copy(
            source.at[:, :, cols], target.at[:, :, cols], sem.at[field, i]
        )

    def send(i):
        dests = pl.ds(i * group, group)
        return pltpu.make_async_copy(out_ref.at[dests], out_hbm.at[dests], out_sem.at[i])

    def tile(ref, a, pair, t):
        return ref[a, :, pl.ds(per_pair * pair + 128 * t, 128)]

    def paired(ref0, a0, ref1, a1, pair, e):
        x, y = tile(ref0, a0, pair, full).astype(F32), tile(ref1, a1, pair, full).astype(F32)
        if e == 0:
            y = pltpu.roll(y, 64, 1)
        else:
            x = pltpu.roll(x, 64, 1)
        return jnp.where(low, x, y).astype(BF16)

    for i in range(steps):
        for field in range(2):
            fetch(field, i).start()
    for i in range(steps):
        for field in range(2):
            fetch(field, i).wait()
        for dest in range(i * group, (i + 1) * group):
            pair, e = dest // 2, dest % 2
            first = e * (full + 1)
            for a in range(parts):
                for t in range(full):
                    out_ref[dest, a * full + t] = tile(disp_ref, a, pair, first + t)
                    out_ref[dest, base + 3 + a * full + t] = tile(force_ref, a, pair, first + t)
            out_ref[dest, base] = paired(disp_ref, 0, disp_ref, 1, pair, e)
            out_ref[dest, base + 1] = paired(disp_ref, 2, force_ref, 2, pair, e)
            out_ref[dest, base + 2] = paired(force_ref, 0, force_ref, 1, pair, e)
        send(i).start()
    for i in range(steps):
        send(i).wait()


def pack(displacements, forces, width):
    parts, configs, atoms = displacements.shape
    per = atoms // width
    steps = 4 if width % 8 == 0 else 1
    tiles = 2 * parts * (per // 128) + 3
    hbm = pl.BlockSpec(memory_space=pltpu.HBM)
    return pl.pallas_call(
        pack_kernel,
        in_specs=[hbm, hbm],
        out_specs=hbm,
        out_shape=shape((width, tiles, configs, 128)),
        scratch_shapes=[VMEM(displacements.shape, BF16)] * 2
        + [VMEM((width, tiles, configs, 128), BF16)]
        + [pltpu.SemaphoreType.DMA((2, steps)), pltpu.SemaphoreType.DMA((steps,))],
        compiler_params=params(8),
        cost_estimate=cost(0, 8 * displacements.size),
    )(*(pltpu.with_memory_space_constraint(x, pltpu.HBM) for x in (displacements, forces)))


def one_hots(index_ref, full):
    index = index_ref[...]
    rows = index.shape[0]
    lane = lax.broadcasted_iota(jnp.int32, (rows, 128), 1)

    def hot(cond):
        return jnp.where(cond, 1.0, 0.0).astype(BF16)

    wholes = [jnp.concatenate([hot(index - 128 * t == lane) for t in range(full)], axis=1)]
    rest = index - 128 * full
    lower = hot(rest == lane)
    upper = hot((rest >= 0) & (rest + 64 == lane))
    return wholes, lower, upper


def picked(whole_hot, half_hot, tiles, half):
    hot = jnp.concatenate([whole_hot, half_hot], axis=1)
    tile = jnp.concatenate([*tiles, half], axis=1)
    return lax.dot_general(hot, tile, NT, preferred_element_type=F32)


def flat(ref, t):
    block = ref[:, t]
    return block.reshape(block.shape[0] * block.shape[1], 128)


def component(recv_ref, hots, field, a):
    (wholes,), lower, upper = hots
    full = wholes.shape[1] // 128
    base = 3 * full
    half = base + 1 if a == 2 else base + 2 * field
    first = a * full + field * (base + 3)
    half_hot = upper if (a == 1 if field == 0 else a > 0) else lower
    tiles = [flat(recv_ref, first + t) for t in range(full)]
    return picked(wholes, half_hot, tiles, flat(recv_ref, half))


def put(out_ref, index_ref, recv_ref, field, dtype):
    clusters, dof, _ = out_ref.shape
    atoms = dof // 3
    hots = one_hots(index_ref, recv_ref.shape[1] // (6 if recv_ref.shape[1] % 3 == 0 else 3))
    for a in range(3):
        got = component(recv_ref, hots, field, a).astype(dtype)
        for c in range(clusters):
            out_ref[c, a * atoms : (a + 1) * atoms] = got[c * atoms : (c + 1) * atoms]


def gather_and_pass_kernel(flag_ref, index_ref, recv_ref, out_ref, pass_ref):
    reach, tiles, configs, _ = pass_ref.shape
    upper = jnp.broadcast_to(flag_ref[0:1] > 0, (configs, 128))
    for i in range(reach):
        for t in range(tiles):
            pass_ref[i, t] = jnp.where(upper, recv_ref[reach + i, t], recv_ref[i, t])
    put(out_ref, index_ref, recv_ref, 0, BF16)


def disp_tiles(recv):
    return 3 * ((recv.shape[1] - 3) // 6) + 2


def gather_and_pass(flags, index, recv, clusters, atoms):
    width, _, configs, _ = recv.shape
    return pl.pallas_call(
        gather_and_pass_kernel,
        in_specs=in_vmem(3),
        out_specs=in_vmem(2),
        out_shape=[
            shape((clusters, 3 * atoms, width * configs)),
            shape((width // 2, disp_tiles(recv), configs, 128)),
        ],
        compiler_params=params(8),
        cost_estimate=cost(recv.size * index.size, 3 * recv.size),
    )(flags, index, recv)


def pick_kernel(route_ref, send_ref, *rest):
    outs, sem = rest[:-1], rest[-1]
    copies = [
        pltpu.make_async_copy(
            send_ref.at[route_ref[0, j], pl.ds(0, out.shape[0])], out, sem.at[j]
        )
        for j, out in enumerate(outs)
    ]
    for copy in copies:
        copy.start()
    for copy in copies:
        copy.wait()


def pick(route, send):
    reach = route.shape[1]
    _, _, configs, _ = send.shape
    return pl.pallas_call(
        pick_kernel,
        in_specs=[in_smem(), pl.BlockSpec(memory_space=pltpu.HBM)],
        out_specs=in_vmem(reach),
        out_shape=[shape((disp_tiles(send), configs, 128))] * reach,
        scratch_shapes=[pltpu.SemaphoreType.DMA((reach,))],
        compiler_params=params(60),
        cost_estimate=cost(0, send.size),
    )(route, pltpu.with_memory_space_constraint(send, pltpu.HBM))


def masked(block_ref, block, c, n, blocks):
    return jnp.where(block_ref[c, n] < blocks, block, jnp.zeros_like(block))


def order_kernel(block_ref, phi_ref, out_ref, held, sem):
    clusters, blocks = phi_ref.shape[:2]
    layer = held.shape[1]

    def fetch(c, n):
        k = jnp.minimum(block_ref[c, 2 * layer + n], blocks - 1)
        return pltpu.make_async_copy(phi_ref.at[c, k], held.at[c, n], sem.at[c, n])

    for c in range(clusters):
        for n in range(layer):
            fetch(c, n).start()
    for c in range(clusters):
        for n in range(layer):
            fetch(c, n).wait()
        row = [masked(block_ref, held[c, n], c, 2 * layer + n, blocks) for n in range(layer)]
        out_ref[c] = jnp.concatenate(row, axis=1)


def ordered(block_of, phi):
    clusters, _, dof, _ = phi.shape
    layer = block_of.shape[1] // 3
    return pl.pallas_call(
        order_kernel,
        in_specs=[in_smem(), pl.BlockSpec(memory_space=pltpu.HBM)],
        out_specs=in_vmem(1)[0],
        out_shape=shape((clusters, dof, layer * dof)),
        scratch_shapes=[
            VMEM((clusters, layer, dof, dof), BF16),
            pltpu.SemaphoreType.DMA((clusters, layer)),
        ],
        compiler_params=params(60),
        cost_estimate=cost(0, 2 * phi.size),
    )(block_of, pltpu.with_memory_space_constraint(phi, pltpu.HBM))


def near_harmonic_kernel(
    block_ref, phi_ref, own_ref, partner_ref, wt_ref, *rest, dense
):
    if dense:
        route_ref, index_ref, recv_ref, *rest = rest
        reach = route_ref.shape[1]
        pieces = rest[:reach]
        out_ref, wdisp_ref, frame_ref, held, block_sem, sem = rest[reach:]
        copies = [
            pltpu.make_async_copy(
                piece, frame_ref.at[lax.rem(route_ref[1, j], reach)], sem.at[j]
            )
            for j, piece in enumerate(pieces)
        ]
    else:
        force_ref, out_ref, wdisp_ref, held, block_sem = rest
        copies = []
    layer = own_ref.shape[0]
    clusters, blocks = phi_ref.shape[:2]

    def fetch(n, c):
        k = jnp.minimum(block_ref[c, n], blocks - 1)
        return pltpu.make_async_copy(phi_ref.at[c, k], held.at[n, c], block_sem.at[n, c])

    for n in range(2 * layer):
        for c in range(clusters):
            fetch(n, c).start()
    for copy in copies:
        copy.start()
    wt = 0.5 * wt_ref[...]
    for c in range(clusters):
        wdisp_ref[c] = (own_ref[c].astype(F32) * wt).astype(BF16)
    if dense:
        put(out_ref, index_ref, recv_ref, 1, F32)
    else:
        out_ref[...] = force_ref[...].astype(F32)
    for n in range(2 * layer):
        for c in range(clusters):
            fetch(n, c).wait()
        left = jnp.concatenate(
            [masked(block_ref, held[n, c], c, n, blocks) for c in range(clusters)], axis=0
        )
        disp = own_ref[n] if n < layer else partner_ref[n - layer]
        got = jnp.dot(left, disp, preferred_element_type=F32)
        out_ref[...] = out_ref[...] + got.reshape(out_ref.shape)
    for copy in copies:
        copy.wait()


def near_harmonic(block_of, phi, own, partner, wt, dense, extra):
    clusters, _, dof, _ = phi.shape
    configs = own.shape[2]
    layer = own.shape[0]
    in_specs = [in_smem(), pl.BlockSpec(memory_space=pltpu.HBM)] + in_vmem(3)
    out_shape = [shape(own.shape, F32), shape(own.shape)]
    scratch = [
        VMEM((2 * layer, clusters, dof, dof), BF16),
        pltpu.SemaphoreType.DMA((2 * layer, clusters)),
    ]
    if dense:
        pieces = extra[3:]
        in_specs += [in_smem()] + in_vmem(2)
        in_specs += [pl.BlockSpec(memory_space=pl.ANY)] * len(pieces)
        out_shape.append(shape((len(pieces), *pieces[0].shape)))
        scratch.append(pltpu.SemaphoreType.DMA((len(pieces),)))
    else:
        in_specs += in_vmem(1)
    return pl.pallas_call(
        functools.partial(near_harmonic_kernel, dense=dense),
        in_specs=in_specs,
        out_specs=in_vmem(len(out_shape)),
        out_shape=out_shape,
        scratch_shapes=scratch,
        compiler_params=params(16),
        cost_estimate=cost(2 * phi.size * configs, 2 * phi.size),
    )(block_of, pltpu.with_memory_space_constraint(phi, pltpu.HBM), own, partner, wt, *extra)


def residual_kernel(phi_ref, far_ref, base_ref, wt_ref, res_ref, wres_ref):
    clusters, _, configs = res_ref.shape
    far = far_ref[...].reshape(phi_ref.shape[2], configs)
    wt = 0.5 * wt_ref[...]
    for c in range(clusters):
        total = base_ref[c] + jnp.dot(phi_ref[c], far, preferred_element_type=F32)
        res = total.astype(BF16)
        res_ref[c] = res
        wres_ref[c] = (res.astype(F32) * wt).astype(BF16)


def residual_of(phi_far, far, base, wt):
    return pl.pallas_call(
        residual_kernel,
        in_specs=in_vmem(4),
        out_specs=in_vmem(2),
        out_shape=[shape(far.shape)] * 2,
        compiler_params=params(8),
        cost_estimate=cost(2 * phi_far.size * far.shape[2], 2 * phi_far.size),
    )(phi_far, far, base, wt)


def merged_residual_kernel(
    flag_ref, index_ref, recv_ref, frame_ref, phi_ref, base_ref, wt_ref, res_ref, wres_ref,
    far_ref, both
):
    reach, tiles, configs, _ = recv_ref.shape
    first = jnp.broadcast_to(flag_ref[1:2] > 0, (configs, 128))
    for i in range(reach):
        for t in range(tiles):
            x, y = frame_ref[i, t], recv_ref[i, t]
            both[i, t] = jnp.where(first, x, y)
            both[reach + i, t] = jnp.where(first, y, x)
    put(far_ref, index_ref, both, 0, BF16)
    residual_kernel(phi_ref, far_ref, base_ref, wt_ref, res_ref, wres_ref)


def merged_residual(flags, index, recv, frame, phi_far, base, wt):
    reach, tiles, configs, _ = recv.shape
    return pl.pallas_call(
        merged_residual_kernel,
        in_specs=in_vmem(7),
        out_specs=in_vmem(3),
        out_shape=[shape(base.shape)] * 3,
        scratch_shapes=[VMEM((2 * reach, tiles, configs, 128), BF16)],
        compiler_params=params(8),
        cost_estimate=cost(
            2 * phi_far.size * base.shape[2] + 2 * recv.size * index.size, 2 * phi_far.size
        ),
    )(flags, index, recv, frame, phi_far, base, wt)


def put_blocks(block_ref, held, out_ref, sem, first):
    clusters, blocks = out_ref.shape[:2]

    def placed(i, c, act):
        k = block_ref[c, first + i]
        copy = pltpu.make_async_copy(
            held.at[i, c], out_ref.at[c, jnp.minimum(k, blocks - 1)], sem.at[i, c]
        )
        pl.when(k < blocks)(getattr(copy, act))

    def start(i):
        for c in range(clusters):
            placed(i, c, "start")

    def finish():
        for i in range(held.shape[0]):
            for c in range(clusters):
                placed(i, c, "wait")

    return start, finish


def near_gradient_kernel(
    block_ref, wres_ref, wdisp_ref, down, dnear, dfar, rown, rnear, out_ref, whole_ref, far_ref,
    held, sem, whole_sem
):
    clusters, dof, configs = wres_ref.shape
    layer = down.shape[0]
    keep = pltpu.make_async_copy(rown, whole_ref, whole_sem)
    keep.start()
    start, finish = put_blocks(block_ref, held, out_ref, sem, 0)
    wres = wres_ref[...].reshape(clusters * dof, configs)
    wdisp = wdisp_ref[...].reshape(clusters * dof, configs)
    left = jnp.concatenate([wres, wdisp], axis=1)
    for i in range(2 * layer):
        disp, res = (down, rown) if i < layer else (dnear, rnear)
        right = jnp.concatenate([disp[i % layer], res[i % layer]], axis=1)
        got = lax.dot_general(left, right, NT, preferred_element_type=F32)
        held[i] = got.astype(BF16).reshape(held.shape[1:])
        start(i)
    for i in range(layer):
        got = lax.dot_general(wres, dfar[i], NT, preferred_element_type=F32)
        far_ref[i] = got.reshape(far_ref.shape[1:])
    finish()
    keep.wait()


def far_gradient_kernel(
    table_ref, wdisp_ref, rfar, far_ref, prior_ref, out_ref, held, sem, block_ref, table_sem
):
    clusters, dof, configs = wdisp_ref.shape
    table = pltpu.make_async_copy(table_ref, block_ref, table_sem)
    table.start()
    start, finish = put_blocks(block_ref, held, out_ref, sem, 2 * far_ref.shape[0])
    left = wdisp_ref[...].reshape(clusters * dof, configs)
    for i in range(rfar.shape[0]):
        got = lax.dot_general(left, rfar[i], NT, preferred_element_type=F32)
        held[i] = (far_ref[i] + got.reshape(held.shape[1:])).astype(BF16)
        if i == 0:
            table.wait()
        start(i)
    finish()


def block_copies(count, clusters, dof):
    return [
        VMEM((count, clusters, dof, dof), BF16),
        pltpu.SemaphoreType.DMA((count, clusters)),
    ]


def near_gradient(block_of, wres, wdisp, fields, out):
    clusters, _, dof, _ = out.shape
    layer = fields[0].shape[0]
    hbm = pl.BlockSpec(memory_space=pltpu.HBM)
    return pl.pallas_call(
        near_gradient_kernel,
        in_specs=[in_smem()] + in_vmem(7),
        out_specs=[hbm, hbm] + in_vmem(1),
        out_shape=[out, shape(wres.shape), shape((layer, clusters, dof, dof), F32)],
        scratch_shapes=block_copies(2 * layer, clusters, dof) + [pltpu.SemaphoreType.DMA(())],
        compiler_params=params(16),
        cost_estimate=cost(10 * layer * dof * wres.size, 4 * layer * clusters * dof * dof),
    )(block_of, wres, wdisp, *fields)


def far_gradient(block_of, wdisp, rfar, far, prior):
    clusters, _, dof, _ = prior.shape
    layer = rfar.shape[0]
    hbm = pl.BlockSpec(memory_space=pltpu.HBM)
    return pl.pallas_call(
        far_gradient_kernel,
        in_specs=in_vmem(4) + [hbm],
        out_specs=hbm,
        out_shape=shape(prior.shape),
        scratch_shapes=block_copies(layer, clusters, dof)
        + [SMEM(block_of.shape, jnp.int32), pltpu.SemaphoreType.DMA(())],
        input_output_aliases={4: 0},
        compiler_params=params(8),
        cost_estimate=cost(2 * layer * dof * wdisp.size, 6 * layer * clusters * dof * dof),
    )(block_of, wdisp, rfar, far, prior)


def swap_near(block):
    count = lax.axis_size("cx")
    return lax.ppermute(block, "cx", [(i, i ^ 1) for i in range(count)])


def swap_far(block):
    count = lax.axis_size("cx")
    pairs = [(i, (i + 1) % count if i % 2 else (i - 1) % count) for i in range(count)]
    return lax.ppermute(block, "cx", pairs)


def far_of(i, count):
    return (i + 2 * (i % 2) - 1) % count


def routes(position, width, reach):
    q = jnp.arange(reach, dtype=jnp.int32)[None, :]
    row = jnp.arange(4, dtype=jnp.int32)[:, None]
    block = position // reach * reach
    far_block = far_of(position, width) // reach * reach
    peer = position ^ q
    rest = (jnp.where(row == 2, block, far_block) + reach + q) % width
    return jnp.where(row == 0, far_of(peer, width), jnp.where(row == 1, peer, rest))


def halves(position, width, reach):
    row = jnp.arange(2, dtype=jnp.int32)[:, None]
    who = jnp.where(row == 0, far_of(position, width), position)
    return jnp.broadcast_to((who < reach).astype(jnp.int32), (2, 128))


def arrange(field, atom_map):
    taken = jnp.take(field, atom_map.reshape(-1), axis=2)
    taken = taken.reshape(field.shape[0], 3, atom_map.shape[0], atom_map.shape[1])
    return jnp.transpose(taken, (2, 1, 3, 0)).reshape(
        atom_map.shape[0], 3 * atom_map.shape[1], field.shape[0]
    )


def tables(neighbours, config_order, weights, layer, position, width):
    blocks = neighbours.shape[1]
    offset = (neighbours // layer - position + 1 + width) % width
    partner = jnp.where(position % 2 == 0, 2, 0)
    group = jnp.where(offset == 1, 0, jnp.where(offset == partner, 1, 2))
    slot = group * layer + neighbours % layer
    named = slot[:, None, :] == jnp.arange(3 * layer, dtype=jnp.int32)[None, :, None]
    block_of = jnp.min(
        jnp.where(named, jnp.arange(blocks, dtype=jnp.int32)[None, None, :], blocks), axis=2
    )
    match = config_order[:, None] == jnp.arange(config_order.shape[0], dtype=jnp.int32)[None, :]
    wt = jnp.sum(jnp.where(match, weights[None, :], 0.0), axis=1)[None, :]
    return block_of, wt


def shards(displacements, forces, phi, neighbours, cluster_atoms, config_order, weights):
    width = lax.axis_size("cx")
    position = lax.axis_index("cx")
    layer, atoms = cluster_atoms.shape
    per = displacements.shape[2] // width
    block_of, wt = tables(neighbours, config_order, weights, layer, position, width)
    atom_local = cluster_atoms - position * per
    reach = width // 2
    dense = displacements.shape[0] % 16 == 0 and per % 128 == 64
    dense = dense and reach & (reach - 1) == 0 and displacements.shape[0] * reach % 128 == 0
    phi_far = ordered(block_of, phi)
    if dense:
        send = pack(
            jnp.transpose(displacements, (1, 0, 2)), jnp.transpose(forces, (1, 0, 2)), width
        )
        recv = lax.all_to_all(send, "cx", split_axis=0, concat_axis=0, tiled=True)
        index = (atom_local - 64 * (position % 2) + per) % per
        route = routes(position, width, reach)
        flags = halves(position, width, reach)
        index_far = swap_far(index).reshape(-1, 1)
        index = index.reshape(-1, 1)
        pieces = list(pick(route, send))
        for j in range(1, reach):
            pieces[j] = lax.ppermute(pieces[j], "cx", [(i, i ^ j) for i in range(width)])
        disp, passed = gather_and_pass(flags, index, recv, layer, atoms)
        recv_far = swap_far(passed)
        extra = (route, index, recv, *pieces)
    else:
        disp, force = (
            arrange(lax.all_to_all(x, "cx", split_axis=2, concat_axis=0, tiled=True), atom_local)
            for x in (displacements, forces)
        )
        disp_far = swap_far(disp)
        extra = (force,)
    disp_near = swap_near(disp)
    base, wdisp, *frame = near_harmonic(block_of, phi, disp, disp_near, wt, dense, extra)
    if dense:
        res, wres, disp_far = merged_residual(
            flags, index_far, recv_far, frame[0], phi_far, base, wt
        )
    else:
        res, wres = residual_of(phi_far, disp_far, base, wt)
    res_far = swap_far(res)
    res_near = swap_near(res)
    gradient, residual, far = near_gradient(
        block_of, wres, wdisp, (disp, disp_near, disp_far, res, res_near), shape(phi.shape)
    )
    return residual, far_gradient(block_of, wdisp, res_far, far, gradient)


def solution(mesh):
    both = ("groups", "cx")
    in_specs = (
        P(both, None, None),
        P(both, None, None),
        P(both, None, None, None),
        P("cx", None),
        P("cx", None),
        P("groups"),
        P("groups"),
    )
    out_specs = (P(both, None, None), P(both, None, None, None))
    return jax.shard_map(shards, mesh=mesh, in_specs=in_specs, out_specs=out_specs, check_vma=False)
```

```python
import functools

import jax
import jax.numpy as jnp
from jax import lax
from jax.experimental import pallas as pl
from jax.experimental.pallas import tpu as pltpu
from jax.sharding import PartitionSpec as P


BF16 = jnp.bfloat16
F32 = jnp.float32
VMEM = pltpu.VMEM
SMEM = pltpu.SMEM
NT = (((1,), (1,)), ((), ()))
MIB = 1024 * 1024


def in_vmem(count):
    return [pl.BlockSpec(memory_space=VMEM)] * count


def in_smem():
    return pl.BlockSpec(memory_space=SMEM)


def params(mib, **kw):
    return pltpu.CompilerParams(vmem_limit_bytes=mib * MIB, **kw)


def cost(flops, nbytes):
    return pl.CostEstimate(flops=flops, bytes_accessed=nbytes, transcendentals=0)


def shape(dims, dtype=BF16):
    return jax.ShapeDtypeStruct(dims, dtype)


def pack_kernel(disp_hbm, force_hbm, out_hbm, disp_ref, force_ref, out_ref, sem, out_sem):
    parts, configs, lanes = disp_ref.shape
    steps = sem.shape[1]
    group = out_ref.shape[0] // steps
    chunk = lanes // steps
    per_pair = 2 * lanes // out_ref.shape[0]
    full = per_pair // 256
    base = parts * full
    low = lax.broadcasted_iota(jnp.int32, (configs, 128), 1) < 64

    def fetch(field, i):
        source, target = ((disp_hbm, disp_ref), (force_hbm, force_ref))[field]
        cols = pl.ds(i * chunk, chunk)
        return pltpu.make_async_copy(
            source.at[:, :, cols], target.at[:, :, cols], sem.at[field, i]
        )

    def send(i):
        dests = pl.ds(i * group, group)
        return pltpu.make_async_copy(out_ref.at[dests], out_hbm.at[dests], out_sem.at[i])

    def tile(ref, a, pair, t):
        return ref[a, :, pl.ds(per_pair * pair + 128 * t, 128)]

    def paired(ref0, a0, ref1, a1, pair, e):
        x, y = tile(ref0, a0, pair, full).astype(F32), tile(ref1, a1, pair, full).astype(F32)
        if e == 0:
            y = pltpu.roll(y, 64, 1)
        else:
            x = pltpu.roll(x, 64, 1)
        return jnp.where(low, x, y).astype(BF16)

    for i in range(steps):
        for field in range(2):
            fetch(field, i).start()
    for i in range(steps):
        for field in range(2):
            fetch(field, i).wait()
        for dest in range(i * group, (i + 1) * group):
            pair, e = dest // 2, dest % 2
            first = e * (full + 1)
            for a in range(parts):
                for t in range(full):
                    out_ref[dest, a * full + t] = tile(disp_ref, a, pair, first + t)
                    out_ref[dest, base + 3 + a * full + t] = tile(force_ref, a, pair, first + t)
            out_ref[dest, base] = paired(disp_ref, 0, disp_ref, 1, pair, e)
            out_ref[dest, base + 1] = paired(disp_ref, 2, force_ref, 2, pair, e)
            out_ref[dest, base + 2] = paired(force_ref, 0, force_ref, 1, pair, e)
        send(i).start()
    for i in range(steps):
        send(i).wait()


def pack(displacements, forces, width):
    parts, configs, atoms = displacements.shape
    per = atoms // width
    steps = 4 if width % 8 == 0 else 1
    tiles = 2 * parts * (per // 128) + 3
    hbm = pl.BlockSpec(memory_space=pltpu.HBM)
    return pl.pallas_call(
        pack_kernel,
        in_specs=[hbm, hbm],
        out_specs=hbm,
        out_shape=shape((width, tiles, configs, 128)),
        scratch_shapes=[VMEM(displacements.shape, BF16)] * 2
        + [VMEM((width, tiles, configs, 128), BF16)]
        + [pltpu.SemaphoreType.DMA((2, steps)), pltpu.SemaphoreType.DMA((steps,))],
        compiler_params=params(8),
        cost_estimate=cost(0, 8 * displacements.size),
    )(*(pltpu.with_memory_space_constraint(x, pltpu.HBM) for x in (displacements, forces)))


def one_hots(index_ref, full):
    index = index_ref[...]
    rows = index.shape[0]
    lane = lax.broadcasted_iota(jnp.int32, (rows, 128), 1)

    def hot(cond):
        return jnp.where(cond, 1.0, 0.0).astype(BF16)

    wholes = [jnp.concatenate([hot(index - 128 * t == lane) for t in range(full)], axis=1)]
    rest = index - 128 * full
    lower = hot(rest == lane)
    upper = hot((rest >= 0) & (rest + 64 == lane))
    return wholes, lower, upper


def picked(whole_hot, half_hot, tiles, half):
    hot = jnp.concatenate([whole_hot, half_hot], axis=1)
    tile = jnp.concatenate([*tiles, half], axis=1)
    return lax.dot_general(hot, tile, NT, preferred_element_type=F32)


def flat(ref, t):
    block = ref[:, t]
    return block.reshape(block.shape[0] * block.shape[1], 128)


def component(recv_ref, hots, field, a):
    (wholes,), lower, upper = hots
    full = wholes.shape[1] // 128
    base = 3 * full
    half = base + 1 if a == 2 else base + 2 * field
    first = a * full + field * (base + 3)
    half_hot = upper if (a == 1 if field == 0 else a > 0) else lower
    tiles = [flat(recv_ref, first + t) for t in range(full)]
    return picked(wholes, half_hot, tiles, flat(recv_ref, half))


def put(out_ref, index_ref, recv_ref, field, dtype):
    clusters, dof, _ = out_ref.shape
    atoms = dof // 3
    hots = one_hots(index_ref, recv_ref.shape[1] // (6 if recv_ref.shape[1] % 3 == 0 else 3))
    for a in range(3):
        got = component(recv_ref, hots, field, a).astype(dtype)
        for c in range(clusters):
            out_ref[c, a * atoms : (a + 1) * atoms] = got[c * atoms : (c + 1) * atoms]


def gather_and_pass_kernel(flag_ref, index_ref, recv_ref, out_ref, pass_ref):
    clusters, dof, half = pass_ref.shape
    put(out_ref, index_ref, recv_ref, 0, BF16)
    upper = jnp.broadcast_to(flag_ref[4:5] > 0, (dof, half))
    for c in range(clusters):
        pass_ref[c] = jnp.where(upper, out_ref[c, :, half:], out_ref[c, :, :half])


def disp_tiles(recv):
    return 3 * ((recv.shape[1] - 3) // 6) + 2


def gather_and_pass(flags, index, recv, clusters, atoms):
    width, _, configs, _ = recv.shape
    whole = (clusters, 3 * atoms, width * configs)
    return pl.pallas_call(
        gather_and_pass_kernel,
        in_specs=in_vmem(3),
        out_specs=in_vmem(2),
        out_shape=[shape(whole), shape((*whole[:2], whole[2] // 2))],
        compiler_params=params(8),
        cost_estimate=cost(recv.size * index.size, 3 * recv.size),
    )(flags, index, recv)


def pick_kernel(route_ref, send_ref, *rest):
    outs, sem = rest[:-1], rest[-1]
    copies = [
        pltpu.make_async_copy(
            send_ref.at[route_ref[0, j], pl.ds(0, out.shape[0])], out, sem.at[j]
        )
        for j, out in enumerate(outs)
    ]
    for copy in copies:
        copy.start()
    for copy in copies:
        copy.wait()


def pick(route, send, reach):
    _, _, configs, _ = send.shape
    return pl.pallas_call(
        pick_kernel,
        in_specs=[in_smem(), pl.BlockSpec(memory_space=pltpu.HBM)],
        out_specs=in_vmem(reach),
        out_shape=[shape((disp_tiles(send), configs, 128))] * reach,
        scratch_shapes=[pltpu.SemaphoreType.DMA((reach,))],
        compiler_params=params(60),
        cost_estimate=cost(0, send.size),
    )(route, pltpu.with_memory_space_constraint(send, pltpu.HBM))


def masked(block_ref, block, c, n, blocks):
    return jnp.where(block_ref[c, n] < blocks, block, jnp.zeros_like(block))


def order_kernel(block_ref, phi_ref, out_ref, held, sem, rows, row_sem):
    clusters, blocks = phi_ref.shape[:2]
    layer = held.shape[1]

    def fetch(c, n):
        k = jnp.minimum(block_ref[c, 2 * layer + n], blocks - 1)
        return pltpu.make_async_copy(phi_ref.at[c, k], held.at[c, n], sem.at[c, n])

    def send(c):
        return pltpu.make_async_copy(rows.at[c], out_ref.at[c], row_sem.at[c])

    for c in range(clusters):
        for n in range(layer):
            fetch(c, n).start()
    for c in range(clusters):
        for n in range(layer):
            fetch(c, n).wait()
        row = [masked(block_ref, held[c, n], c, 2 * layer + n, blocks) for n in range(layer)]
        rows[c] = jnp.concatenate(row, axis=1)
        send(c).start()
    for c in range(clusters):
        send(c).wait()


def ordered(block_of, phi):
    clusters, _, dof, _ = phi.shape
    layer = block_of.shape[1] // 3
    hbm = pl.BlockSpec(memory_space=pltpu.HBM)
    return pl.pallas_call(
        order_kernel,
        in_specs=[in_smem(), hbm],
        out_specs=hbm,
        out_shape=shape((clusters, dof, layer * dof)),
        scratch_shapes=[
            VMEM((clusters, layer, dof, dof), BF16),
            pltpu.SemaphoreType.DMA((clusters, layer)),
            VMEM((clusters, dof, layer * dof), BF16),
            pltpu.SemaphoreType.DMA((clusters,)),
        ],
        compiler_params=params(60),
        cost_estimate=cost(0, 2 * phi.size),
    )(block_of, pltpu.with_memory_space_constraint(phi, pltpu.HBM))


def near_harmonic_kernel(
    block_ref, phi_ref, own_ref, partner_ref, wt_ref, *rest, dense
):
    if dense:
        route_ref, index_ref, recv_ref, index_far_ref, *rest = rest
        pieces, (out_ref, wdisp_ref, far_ref, held, block_sem, frame, sem) = rest[:-7], rest[-7:]
        reach = len(pieces)
        copies = [
            pltpu.make_async_copy(
                piece, frame.at[lax.rem(route_ref[1, j], reach)], sem.at[j]
            )
            for j, piece in enumerate(pieces)
        ]
    else:
        force_ref, out_ref, wdisp_ref, held, block_sem = rest
        copies = []
    layer = own_ref.shape[0]
    clusters, blocks = phi_ref.shape[:2]

    def fetch(n, c):
        k = jnp.minimum(block_ref[c, n], blocks - 1)
        return pltpu.make_async_copy(phi_ref.at[c, k], held.at[n, c], block_sem.at[n, c])

    for copy in copies:
        copy.start()
    for n in range(2 * layer):
        for c in range(clusters):
            fetch(n, c).start()
    wt = 0.5 * wt_ref[...]
    for c in range(clusters):
        wdisp_ref[c] = (own_ref[c].astype(F32) * wt).astype(BF16)
    if dense:
        put(out_ref, index_ref, recv_ref, 1, F32)
        for copy in copies:
            copy.wait()
        put(far_ref, index_far_ref, frame, 0, BF16)
    else:
        out_ref[...] = force_ref[...].astype(F32)
    for n in range(2 * layer):
        for c in range(clusters):
            fetch(n, c).wait()
        left = jnp.concatenate(
            [masked(block_ref, held[n, c], c, n, blocks) for c in range(clusters)], axis=0
        )
        disp = own_ref[n] if n < layer else partner_ref[n - layer]
        got = jnp.dot(left, disp, preferred_element_type=F32)
        out_ref[...] = out_ref[...] + got.reshape(out_ref.shape)


def near_harmonic(block_of, phi, own, partner, wt, dense, extra):
    clusters, _, dof, _ = phi.shape
    configs = own.shape[2]
    layer = own.shape[0]
    in_specs = [in_smem(), pl.BlockSpec(memory_space=pltpu.HBM)] + in_vmem(3)
    out_shape = [shape(own.shape, F32), shape(own.shape)]
    scratch = [
        VMEM((2 * layer, clusters, dof, dof), BF16),
        pltpu.SemaphoreType.DMA((2 * layer, clusters)),
    ]
    if dense:
        pieces = extra[4:]
        in_specs += [in_smem()] + in_vmem(3)
        in_specs += [pl.BlockSpec(memory_space=pl.ANY)] * len(pieces)
        out_shape.append(shape((clusters, dof, configs // 2)))
        scratch.append(VMEM((len(pieces), *pieces[0].shape), BF16))
        scratch.append(pltpu.SemaphoreType.DMA((len(pieces),)))
    else:
        in_specs += in_vmem(1)
    return pl.pallas_call(
        functools.partial(near_harmonic_kernel, dense=dense),
        in_specs=in_specs,
        out_specs=in_vmem(len(out_shape)),
        out_shape=out_shape,
        scratch_shapes=scratch,
        compiler_params=params(16),
        cost_estimate=cost(2 * phi.size * configs, 2 * phi.size),
    )(block_of, pltpu.with_memory_space_constraint(phi, pltpu.HBM), own, partner, wt, *extra)


def pieces_of(dims):
    split = (dims[0] + 1) // 2
    return [shape((split, *dims[1:])), shape((dims[0] - split, *dims[1:]))]


def residual_kernel(phi_ref, far_ref, base_ref, wt_ref, res_ref, wres_ref, a_ref, b_ref):
    clusters, _, configs = res_ref.shape
    far = far_ref[...].reshape(phi_ref.shape[2], configs)
    wt = 0.5 * wt_ref[...]
    for c in range(clusters):
        total = base_ref[c] + jnp.dot(phi_ref[c], far, preferred_element_type=F32)
        res = total.astype(BF16)
        res_ref[c] = res
        if c < a_ref.shape[0]:
            a_ref[c] = res
        else:
            b_ref[c - a_ref.shape[0]] = res
        wres_ref[c] = (res.astype(F32) * wt).astype(BF16)


def residual_of(phi_far, far, base, wt):
    return pl.pallas_call(
        residual_kernel,
        in_specs=in_vmem(4),
        out_specs=in_vmem(4),
        out_shape=[shape(far.shape)] * 2 + pieces_of(far.shape),
        compiler_params=params(8),
        cost_estimate=cost(2 * phi_far.size * far.shape[2], 2 * phi_far.size),
    )(phi_far, far, base, wt)


def merged_residual_kernel(
    flag_ref, recv_ref, direct_ref, phi_ref, base_ref, wt_ref, res_ref, wres_ref, a_ref, b_ref,
    far_ref
):
    clusters, dof, half = recv_ref.shape
    first = jnp.broadcast_to(flag_ref[5:6] > 0, (dof, half))
    for c in range(clusters):
        x, y = direct_ref[c], recv_ref[c]
        far_ref[c, :, :half] = jnp.where(first, x, y)
        far_ref[c, :, half:] = jnp.where(first, y, x)
    residual_kernel(phi_ref, far_ref, base_ref, wt_ref, res_ref, wres_ref, a_ref, b_ref)


def merged_residual(flags, recv, direct, phi_far, base, wt):
    return pl.pallas_call(
        merged_residual_kernel,
        in_specs=in_vmem(6),
        out_specs=in_vmem(5),
        out_shape=[shape(base.shape)] * 2 + pieces_of(base.shape) + [shape(base.shape)],
        compiler_params=params(8),
        cost_estimate=cost(2 * phi_far.size * base.shape[2], 2 * phi_far.size),
    )(flags, recv, direct, phi_far, base, wt)


def put_blocks(block_ref, held, out_ref, sem, first):
    clusters, blocks = out_ref.shape[:2]

    def placed(i, c, act):
        k = block_ref[c, first + i]
        copy = pltpu.make_async_copy(
            held.at[i, c], out_ref.at[c, jnp.minimum(k, blocks - 1)], sem.at[i, c]
        )
        pl.when(k < blocks)(getattr(copy, act))

    def start(i):
        for c in range(clusters):
            placed(i, c, "start")

    def finish():
        for i in range(held.shape[0]):
            for c in range(clusters):
                placed(i, c, "wait")

    return start, finish


def near_gradient_kernel(
    block_ref, wres_ref, wdisp_ref, down, dnear, dfar, rown, rnear, out_ref, whole_ref, far_ref,
    held, sem, whole_sem
):
    clusters, dof, configs = wres_ref.shape
    layer = down.shape[0]
    keep = pltpu.make_async_copy(rown, whole_ref, whole_sem)
    keep.start()
    start, finish = put_blocks(block_ref, held, out_ref, sem, 0)
    wres = wres_ref[...].reshape(clusters * dof, configs)
    wdisp = wdisp_ref[...].reshape(clusters * dof, configs)
    left = jnp.concatenate([wres, wdisp], axis=1)
    for i in range(2 * layer):
        disp, res = (down, rown) if i < layer else (dnear, rnear)
        right = jnp.concatenate([disp[i % layer], res[i % layer]], axis=1)
        first = i if i < layer else 0
        got = lax.dot_general(left[first * dof :], right, NT, preferred_element_type=F32)
        for c in range(first, clusters):
            block = got[(c - first) * dof : (c - first + 1) * dof]
            held[i, c] = block.astype(BF16)
            if i < layer and c > i:
                held[c, i] = block.T.astype(BF16)
        start(i)
    for i in range(layer):
        got = lax.dot_general(wres, dfar[i], NT, preferred_element_type=F32)
        far_ref[i] = got.reshape(far_ref.shape[1:])
    finish()
    keep.wait()


def far_gradient_kernel(
    first, table_ref, wdisp_ref, rfar, far_ref, prior_ref, out_ref, held, sem, block_ref, table_sem
):
    clusters, dof, configs = wdisp_ref.shape
    table = pltpu.make_async_copy(table_ref, block_ref, table_sem)
    table.start()
    start, finish = put_blocks(block_ref, held, out_ref, sem, 2 * far_ref.shape[0] + first)
    left = wdisp_ref[...].reshape(clusters * dof, configs)
    for i in range(rfar.shape[0]):
        got = lax.dot_general(left, rfar[i], NT, preferred_element_type=F32)
        held[i] = (far_ref[first + i] + got.reshape(held.shape[1:])).astype(BF16)
        if i == 0:
            table.wait()
        start(i)
    finish()


def block_copies(count, clusters, dof):
    return [
        VMEM((count, clusters, dof, dof), BF16),
        pltpu.SemaphoreType.DMA((count, clusters)),
    ]


def near_gradient(block_of, wres, wdisp, fields, out):
    clusters, _, dof, _ = out.shape
    layer = fields[0].shape[0]
    hbm = pl.BlockSpec(memory_space=pltpu.HBM)
    return pl.pallas_call(
        near_gradient_kernel,
        in_specs=[in_smem()] + in_vmem(7),
        out_specs=[hbm, hbm] + in_vmem(1),
        out_shape=[out, shape(wres.shape), shape((layer, clusters, dof, dof), F32)],
        scratch_shapes=block_copies(2 * layer, clusters, dof) + [pltpu.SemaphoreType.DMA(())],
        compiler_params=params(16),
        cost_estimate=cost(10 * layer * dof * wres.size, 4 * layer * clusters * dof * dof),
    )(block_of, wres, wdisp, *fields)


def far_gradient(block_of, wdisp, rfar, far, prior, first):
    clusters, _, dof, _ = prior.shape
    layer = rfar.shape[0]
    hbm = pl.BlockSpec(memory_space=pltpu.HBM)
    return pl.pallas_call(
        functools.partial(far_gradient_kernel, first),
        in_specs=in_vmem(4) + [hbm],
        out_specs=hbm,
        out_shape=shape(prior.shape),
        scratch_shapes=block_copies(layer, clusters, dof)
        + [SMEM(block_of.shape, jnp.int32), pltpu.SemaphoreType.DMA(())],
        input_output_aliases={4: 0},
        compiler_params=params(8),
        cost_estimate=cost(2 * layer * dof * wdisp.size, 6 * layer * clusters * dof * dof),
    )(block_of, wdisp, rfar, far, prior)


def swap_near(block):
    count = lax.axis_size("cx")
    return lax.ppermute(block, "cx", [(i, i ^ 1) for i in range(count)])


def swap_far(block):
    count = lax.axis_size("cx")
    pairs = [(i, (i + 1) % count if i % 2 else (i - 1) % count) for i in range(count)]
    return lax.ppermute(block, "cx", pairs)


def far_of(i, count):
    return (i + 2 * (i % 2) - 1) % count


def routes(position, width, reach):
    q = lax.broadcasted_iota(jnp.int32, (8, 128), 1)
    row = lax.broadcasted_iota(jnp.int32, (8, 128), 0)
    peer = position ^ q
    who = jnp.where(row == 4, far_of(position, width), position)
    flag = (who < reach).astype(jnp.int32)
    return jnp.where(row == 0, far_of(peer, width), jnp.where(row == 1, peer, flag))


def arrange(field, atom_map):
    taken = jnp.take(field, atom_map.reshape(-1), axis=2)
    taken = taken.reshape(field.shape[0], 3, atom_map.shape[0], atom_map.shape[1])
    return jnp.transpose(taken, (2, 1, 3, 0)).reshape(
        atom_map.shape[0], 3 * atom_map.shape[1], field.shape[0]
    )


def tables(neighbours, config_order, weights, layer, position, width):
    blocks = neighbours.shape[1]
    offset = (neighbours // layer - position + 1 + width) % width
    partner = jnp.where(position % 2 == 0, 2, 0)
    group = jnp.where(offset == 1, 0, jnp.where(offset == partner, 1, 2))
    slot = group * layer + neighbours % layer
    named = slot[:, None, :] == jnp.arange(3 * layer, dtype=jnp.int32)[None, :, None]
    block_of = jnp.min(
        jnp.where(named, jnp.arange(blocks, dtype=jnp.int32)[None, None, :], blocks), axis=2
    )
    match = config_order[:, None] == jnp.arange(config_order.shape[0], dtype=jnp.int32)[None, :]
    wt = jnp.sum(jnp.where(match, weights[None, :], 0.0), axis=1)[None, :]
    return block_of, wt


def shards(displacements, forces, phi, neighbours, cluster_atoms, config_order, weights):
    width = lax.axis_size("cx")
    position = lax.axis_index("cx")
    layer, atoms = cluster_atoms.shape
    per = displacements.shape[2] // width
    block_of, wt = tables(neighbours, config_order, weights, layer, position, width)
    atom_local = cluster_atoms - position * per
    reach = width // 2
    dense = displacements.shape[0] % 16 == 0 and per % 128 == 64
    dense = dense and reach & (reach - 1) == 0 and displacements.shape[0] * reach % 128 == 0
    phi_far = ordered(block_of, phi)
    if dense:
        send = pack(
            jnp.transpose(displacements, (1, 0, 2)), jnp.transpose(forces, (1, 0, 2)), width
        )
        recv = lax.all_to_all(send, "cx", split_axis=0, concat_axis=0, tiled=True)
        index = (atom_local - 64 * (position % 2) + per) % per
        flags = routes(position, width, reach)
        index_far = swap_far(index).reshape(-1, 1)
        index = index.reshape(-1, 1)
        pieces = list(pick(flags, send, reach))
        for j in range(1, reach):
            pieces[j] = lax.ppermute(pieces[j], "cx", [(i, i ^ j) for i in range(width)])
        disp, passed = gather_and_pass(flags, index, recv, layer, atoms)
        recv_far = swap_far(passed)
        extra = (flags, index, recv, index_far, *pieces)
    else:
        disp, force = (
            arrange(lax.all_to_all(x, "cx", split_axis=2, concat_axis=0, tiled=True), atom_local)
            for x in (displacements, forces)
        )
        disp_far = swap_far(disp)
        extra = (force,)
    disp_near = swap_near(disp)
    base, wdisp, *direct = near_harmonic(block_of, phi, disp, disp_near, wt, dense, extra)
    if dense:
        res, wres, part_a, part_b, disp_far = merged_residual(
            flags, recv_far, direct[0], phi_far, base, wt
        )
    else:
        res, wres, part_a, part_b = residual_of(phi_far, disp_far, base, wt)
    split = part_a.shape[0]
    res_far = swap_far(part_a)
    res_rest = swap_far(part_b)
    res_near = swap_near(res)
    gradient, residual, far = near_gradient(
        block_of, wres, wdisp, (disp, disp_near, disp_far, res, res_near), shape(phi.shape)
    )
    gradient = far_gradient(block_of, wdisp, res_far, far, gradient, 0)
    return residual, far_gradient(block_of, wdisp, res_rest, far, gradient, split)


def solution(mesh):
    both = ("groups", "cx")
    in_specs = (
        P(both, None, None),
        P(both, None, None),
        P(both, None, None, None),
        P("cx", None),
        P("cx", None),
        P("groups"),
        P("groups"),
    )
    out_specs = (P(both, None, None), P(both, None, None, None))
    return jax.shard_map(shards, mesh=mesh, in_specs=in_specs, out_specs=out_specs, check_vma=False)
```

```python
import functools

import jax
import jax.numpy as jnp
from jax import lax
from jax.experimental import pallas as pl
from jax.experimental.pallas import tpu as pltpu
from jax.sharding import PartitionSpec as P


BF16 = jnp.bfloat16
F32 = jnp.float32
VMEM = pltpu.VMEM
SMEM = pltpu.SMEM
NT = (((1,), (1,)), ((), ()))
MIB = 1024 * 1024


def in_vmem(count):
    return [pl.BlockSpec(memory_space=VMEM)] * count


def in_smem():
    return pl.BlockSpec(memory_space=SMEM)


def params(mib, **kw):
    return pltpu.CompilerParams(vmem_limit_bytes=mib * MIB, **kw)


def cost(flops, nbytes):
    return pl.CostEstimate(flops=flops, bytes_accessed=nbytes, transcendentals=0)


def shape(dims, dtype=BF16):
    return jax.ShapeDtypeStruct(dims, dtype)


def pack_kernel(disp_hbm, force_hbm, out_hbm, disp_ref, force_ref, out_ref, sem, out_sem):
    parts, configs, lanes = disp_ref.shape
    steps = sem.shape[1]
    group = out_ref.shape[0] // steps
    chunk = lanes // steps
    per_pair = 2 * lanes // out_ref.shape[0]
    full = per_pair // 256
    base = parts * full
    low = lax.broadcasted_iota(jnp.int32, (configs, 128), 1) < 64

    def fetch(field, i):
        source, target = ((disp_hbm, disp_ref), (force_hbm, force_ref))[field]
        cols = pl.ds(i * chunk, chunk)
        return pltpu.make_async_copy(
            source.at[:, :, cols], target.at[:, :, cols], sem.at[field, i]
        )

    def send(i):
        dests = pl.ds(i * group, group)
        return pltpu.make_async_copy(out_ref.at[dests], out_hbm.at[dests], out_sem.at[i])

    def tile(ref, a, pair, t):
        return ref[a, :, pl.ds(per_pair * pair + 128 * t, 128)]

    def paired(ref0, a0, ref1, a1, pair, e):
        x, y = tile(ref0, a0, pair, full).astype(F32), tile(ref1, a1, pair, full).astype(F32)
        if e == 0:
            y = pltpu.roll(y, 64, 1)
        else:
            x = pltpu.roll(x, 64, 1)
        return jnp.where(low, x, y).astype(BF16)

    for i in range(steps):
        for field in range(2):
            fetch(field, i).start()
    for i in range(steps):
        for field in range(2):
            fetch(field, i).wait()
        for dest in range(i * group, (i + 1) * group):
            pair, e = dest // 2, dest % 2
            first = e * (full + 1)
            for a in range(parts):
                for t in range(full):
                    out_ref[dest, a * full + t] = tile(disp_ref, a, pair, first + t)
                    out_ref[dest, base + 3 + a * full + t] = tile(force_ref, a, pair, first + t)
            out_ref[dest, base] = paired(disp_ref, 0, disp_ref, 1, pair, e)
            out_ref[dest, base + 1] = paired(disp_ref, 2, force_ref, 2, pair, e)
            out_ref[dest, base + 2] = paired(force_ref, 0, force_ref, 1, pair, e)
        send(i).start()
    for i in range(steps):
        send(i).wait()


def pack(displacements, forces, width):
    parts, configs, atoms = displacements.shape
    per = atoms // width
    steps = 4 if width % 8 == 0 else 1
    tiles = 2 * parts * (per // 128) + 3
    hbm = pl.BlockSpec(memory_space=pltpu.HBM)
    return pl.pallas_call(
        pack_kernel,
        in_specs=[hbm, hbm],
        out_specs=hbm,
        out_shape=shape((width, tiles, configs, 128)),
        scratch_shapes=[VMEM(displacements.shape, BF16)] * 2
        + [VMEM((width, tiles, configs, 128), BF16)]
        + [pltpu.SemaphoreType.DMA((2, steps)), pltpu.SemaphoreType.DMA((steps,))],
        compiler_params=params(8),
        cost_estimate=cost(0, 8 * displacements.size),
    )(*(pltpu.with_memory_space_constraint(x, pltpu.HBM) for x in (displacements, forces)))


def one_hots(index_ref, full):
    index = index_ref[...]
    rows = index.shape[0]
    lane = lax.broadcasted_iota(jnp.int32, (rows, 128), 1)

    def hot(cond):
        return jnp.where(cond, 1.0, 0.0).astype(BF16)

    wholes = [jnp.concatenate([hot(index - 128 * t == lane) for t in range(full)], axis=1)]
    rest = index - 128 * full
    lower = hot(rest == lane)
    upper = hot((rest >= 0) & (rest + 64 == lane))
    return wholes, lower, upper


def picked(whole_hot, half_hot, tiles, half):
    hot = jnp.concatenate([whole_hot, half_hot], axis=1)
    tile = jnp.concatenate([*tiles, half], axis=1)
    return lax.dot_general(hot, tile, NT, preferred_element_type=F32)


def flat(ref, t):
    block = ref[:, t]
    return block.reshape(block.shape[0] * block.shape[1], 128)


def component(recv_ref, hots, field, a):
    (wholes,), lower, upper = hots
    full = wholes.shape[1] // 128
    base = 3 * full
    half = base + 1 if a == 2 else base + 2 * field
    first = a * full + field * (base + 3)
    half_hot = upper if (a == 1 if field == 0 else a > 0) else lower
    tiles = [flat(recv_ref, first + t) for t in range(full)]
    return picked(wholes, half_hot, tiles, flat(recv_ref, half))


def put(out_ref, index_ref, recv_ref, field, dtype):
    clusters, dof, _ = out_ref.shape
    atoms = dof // 3
    hots = one_hots(index_ref, recv_ref.shape[1] // (6 if recv_ref.shape[1] % 3 == 0 else 3))
    for a in range(3):
        got = component(recv_ref, hots, field, a).astype(dtype)
        for c in range(clusters):
            out_ref[c, a * atoms : (a + 1) * atoms] = got[c * atoms : (c + 1) * atoms]


def gather_and_pass_kernel(flag_ref, index_ref, recv_ref, out_ref, pass_ref):
    clusters, dof, half = pass_ref.shape
    put(out_ref, index_ref, recv_ref, 0, BF16)
    upper = jnp.broadcast_to(flag_ref[4:5] > 0, (dof, half))
    for c in range(clusters):
        pass_ref[c] = jnp.where(upper, out_ref[c, :, half:], out_ref[c, :, :half])


def disp_tiles(recv):
    return 3 * ((recv.shape[1] - 3) // 6) + 2


def gather_and_pass(flags, index, recv, clusters, atoms):
    width, _, configs, _ = recv.shape
    whole = (clusters, 3 * atoms, width * configs)
    return pl.pallas_call(
        gather_and_pass_kernel,
        in_specs=in_vmem(3),
        out_specs=in_vmem(2),
        out_shape=[shape(whole), shape((*whole[:2], whole[2] // 2))],
        compiler_params=params(8),
        cost_estimate=cost(recv.size * index.size, 3 * recv.size),
    )(flags, index, recv)


def pick_kernel(route_ref, send_ref, *rest):
    outs, sem = rest[:-1], rest[-1]
    copies = [
        pltpu.make_async_copy(
            send_ref.at[route_ref[0, j], pl.ds(0, out.shape[0])], out, sem.at[j]
        )
        for j, out in enumerate(outs)
    ]
    for copy in copies:
        copy.start()
    for copy in copies:
        copy.wait()


def pick(route, send, reach):
    _, _, configs, _ = send.shape
    return pl.pallas_call(
        pick_kernel,
        in_specs=[in_smem(), pl.BlockSpec(memory_space=pltpu.HBM)],
        out_specs=in_vmem(reach),
        out_shape=[shape((disp_tiles(send), configs, 128))] * reach,
        scratch_shapes=[pltpu.SemaphoreType.DMA((reach,))],
        compiler_params=params(60),
        cost_estimate=cost(0, send.size),
    )(route, pltpu.with_memory_space_constraint(send, pltpu.HBM))


def masked(block_ref, block, c, n, blocks):
    return jnp.where(block_ref[c, n] < blocks, block, jnp.zeros_like(block))


def order_kernel(block_ref, phi_ref, out_ref, held, sem, rows, row_sem):
    clusters, blocks = phi_ref.shape[:2]
    layer = held.shape[1]

    def fetch(c, n):
        k = jnp.minimum(block_ref[c, 2 * layer + n], blocks - 1)
        return pltpu.make_async_copy(phi_ref.at[c, k], held.at[c, n], sem.at[c, n])

    def send(c):
        return pltpu.make_async_copy(rows.at[c], out_ref.at[c], row_sem.at[c])

    for c in range(clusters):
        for n in range(layer):
            fetch(c, n).start()
    for c in range(clusters):
        for n in range(layer):
            fetch(c, n).wait()
        row = [masked(block_ref, held[c, n], c, 2 * layer + n, blocks) for n in range(layer)]
        rows[c] = jnp.concatenate(row, axis=1)
        send(c).start()
    for c in range(clusters):
        send(c).wait()


def ordered(block_of, phi):
    clusters, _, dof, _ = phi.shape
    layer = block_of.shape[1] // 3
    hbm = pl.BlockSpec(memory_space=pltpu.HBM)
    return pl.pallas_call(
        order_kernel,
        in_specs=[in_smem(), hbm],
        out_specs=hbm,
        out_shape=shape((clusters, dof, layer * dof)),
        scratch_shapes=[
            VMEM((clusters, layer, dof, dof), BF16),
            pltpu.SemaphoreType.DMA((clusters, layer)),
            VMEM((clusters, dof, layer * dof), BF16),
            pltpu.SemaphoreType.DMA((clusters,)),
        ],
        compiler_params=params(60),
        cost_estimate=cost(0, 2 * phi.size),
    )(block_of, pltpu.with_memory_space_constraint(phi, pltpu.HBM))


def near_harmonic_kernel(
    block_ref, phi_ref, own_ref, partner_ref, wt_ref, *rest, dense
):
    if dense:
        route_ref, index_ref, recv_ref, index_far_ref, *rest = rest
        pieces, (out_ref, wdisp_ref, far_ref, held, block_sem, frame, sem) = rest[:-7], rest[-7:]
        reach = len(pieces)
        copies = [
            pltpu.make_async_copy(
                piece, frame.at[lax.rem(route_ref[1, j], reach)], sem.at[j]
            )
            for j, piece in enumerate(pieces)
        ]
    else:
        force_ref, out_ref, wdisp_ref, held, block_sem = rest
        copies = []
    layer = own_ref.shape[0]
    clusters, blocks = phi_ref.shape[:2]

    def fetch(n, c):
        k = jnp.minimum(block_ref[c, n], blocks - 1)
        return pltpu.make_async_copy(phi_ref.at[c, k], held.at[n, c], block_sem.at[n, c])

    for n in range(2 * layer):
        for c in range(clusters):
            fetch(n, c).start()
    for copy in copies:
        copy.start()
    wt = 0.5 * wt_ref[...]
    for c in range(clusters):
        wdisp_ref[c] = (own_ref[c].astype(F32) * wt).astype(BF16)
    if dense:
        put(out_ref, index_ref, recv_ref, 1, F32)
    else:
        out_ref[...] = force_ref[...].astype(F32)
    for n in range(2 * layer):
        for c in range(clusters):
            fetch(n, c).wait()
        left = jnp.concatenate(
            [masked(block_ref, held[n, c], c, n, blocks) for c in range(clusters)], axis=0
        )
        disp = own_ref[n] if n < layer else partner_ref[n - layer]
        got = jnp.dot(left, disp, preferred_element_type=F32)
        out_ref[...] = out_ref[...] + got.reshape(out_ref.shape)
    for copy in copies:
        copy.wait()
    if dense:
        put(far_ref, index_far_ref, frame, 0, BF16)


def near_harmonic(block_of, phi, own, partner, wt, dense, extra):
    clusters, _, dof, _ = phi.shape
    configs = own.shape[2]
    layer = own.shape[0]
    in_specs = [in_smem(), pl.BlockSpec(memory_space=pltpu.HBM)] + in_vmem(3)
    out_shape = [shape(own.shape, F32), shape(own.shape)]
    scratch = [
        VMEM((2 * layer, clusters, dof, dof), BF16),
        pltpu.SemaphoreType.DMA((2 * layer, clusters)),
    ]
    if dense:
        pieces = extra[4:]
        in_specs += [in_smem()] + in_vmem(3)
        in_specs += [pl.BlockSpec(memory_space=pl.ANY)] * len(pieces)
        out_shape.append(shape((clusters, dof, configs // 2)))
        scratch.append(VMEM((len(pieces), *pieces[0].shape), BF16))
        scratch.append(pltpu.SemaphoreType.DMA((len(pieces),)))
    else:
        in_specs += in_vmem(1)
    return pl.pallas_call(
        functools.partial(near_harmonic_kernel, dense=dense),
        in_specs=in_specs,
        out_specs=in_vmem(len(out_shape)),
        out_shape=out_shape,
        scratch_shapes=scratch,
        compiler_params=params(16),
        cost_estimate=cost(2 * phi.size * configs, 2 * phi.size),
    )(block_of, pltpu.with_memory_space_constraint(phi, pltpu.HBM), own, partner, wt, *extra)


def residual_kernel(phi_ref, far_ref, base_ref, wt_ref, res_ref, wres_ref):
    clusters, _, configs = res_ref.shape
    far = far_ref[...].reshape(phi_ref.shape[2], configs)
    wt = 0.5 * wt_ref[...]
    for c in range(clusters):
        total = base_ref[c] + jnp.dot(phi_ref[c], far, preferred_element_type=F32)
        res = total.astype(BF16)
        res_ref[c] = res
        wres_ref[c] = (res.astype(F32) * wt).astype(BF16)


def residual_of(phi_far, far, base, wt):
    return pl.pallas_call(
        residual_kernel,
        in_specs=in_vmem(4),
        out_specs=in_vmem(2),
        out_shape=[shape(far.shape)] * 2,
        compiler_params=params(8),
        cost_estimate=cost(2 * phi_far.size * far.shape[2], 2 * phi_far.size),
    )(phi_far, far, base, wt)


def merged_residual_kernel(
    flag_ref, recv_ref, direct_ref, phi_ref, base_ref, wt_ref, res_ref, wres_ref, far_ref
):
    clusters, dof, half = recv_ref.shape
    first = jnp.broadcast_to(flag_ref[5:6] > 0, (dof, half))
    for c in range(clusters):
        x, y = direct_ref[c], recv_ref[c]
        far_ref[c, :, :half] = jnp.where(first, x, y)
        far_ref[c, :, half:] = jnp.where(first, y, x)
    residual_kernel(phi_ref, far_ref, base_ref, wt_ref, res_ref, wres_ref)


def merged_residual(flags, recv, direct, phi_far, base, wt):
    return pl.pallas_call(
        merged_residual_kernel,
        in_specs=in_vmem(6),
        out_specs=in_vmem(3),
        out_shape=[shape(base.shape)] * 3,
        compiler_params=params(8),
        cost_estimate=cost(2 * phi_far.size * base.shape[2], 2 * phi_far.size),
    )(flags, recv, direct, phi_far, base, wt)


def put_blocks(block_ref, held, out_ref, sem, first):
    clusters, blocks = out_ref.shape[:2]

    def placed(i, c, act):
        k = block_ref[c, first + i]
        copy = pltpu.make_async_copy(
            held.at[i, c], out_ref.at[c, jnp.minimum(k, blocks - 1)], sem.at[i, c]
        )
        pl.when(k < blocks)(getattr(copy, act))

    def start(i):
        for c in range(clusters):
            placed(i, c, "start")

    def finish():
        for i in range(held.shape[0]):
            for c in range(clusters):
                placed(i, c, "wait")

    return start, finish


def near_gradient_kernel(
    block_ref, wres_ref, wdisp_ref, down, dnear, dfar, rown, rnear, out_ref, whole_ref, far_ref,
    held, sem, whole_sem
):
    clusters, dof, configs = wres_ref.shape
    layer = down.shape[0]
    keep = pltpu.make_async_copy(rown, whole_ref, whole_sem)
    keep.start()
    start, finish = put_blocks(block_ref, held, out_ref, sem, 0)
    wres = wres_ref[...].reshape(clusters * dof, configs)
    wdisp = wdisp_ref[...].reshape(clusters * dof, configs)
    left = jnp.concatenate([wres, wdisp], axis=1)
    for i in range(2 * layer):
        disp, res = (down, rown) if i < layer else (dnear, rnear)
        right = jnp.concatenate([disp[i % layer], res[i % layer]], axis=1)
        got = lax.dot_general(left, right, NT, preferred_element_type=F32)
        held[i] = got.astype(BF16).reshape(held.shape[1:])
        start(i)
    for i in range(layer):
        got = lax.dot_general(wres, dfar[i], NT, preferred_element_type=F32)
        far_ref[i] = got.reshape(far_ref.shape[1:])
    finish()
    keep.wait()


def far_gradient_kernel(
    table_ref, wdisp_ref, rfar, far_ref, prior_ref, out_ref, held, sem, block_ref, table_sem
):
    clusters, dof, configs = wdisp_ref.shape
    table = pltpu.make_async_copy(table_ref, block_ref, table_sem)
    table.start()
    start, finish = put_blocks(block_ref, held, out_ref, sem, 2 * far_ref.shape[0])
    left = wdisp_ref[...].reshape(clusters * dof, configs)
    for i in range(rfar.shape[0]):
        got = lax.dot_general(left, rfar[i], NT, preferred_element_type=F32)
        held[i] = (far_ref[i] + got.reshape(held.shape[1:])).astype(BF16)
        if i == 0:
            table.wait()
        start(i)
    finish()


def block_copies(count, clusters, dof):
    return [
        VMEM((count, clusters, dof, dof), BF16),
        pltpu.SemaphoreType.DMA((count, clusters)),
    ]


def near_gradient(block_of, wres, wdisp, fields, out):
    clusters, _, dof, _ = out.shape
    layer = fields[0].shape[0]
    hbm = pl.BlockSpec(memory_space=pltpu.HBM)
    return pl.pallas_call(
        near_gradient_kernel,
        in_specs=[in_smem()] + in_vmem(7),
        out_specs=[hbm, hbm] + in_vmem(1),
        out_shape=[out, shape(wres.shape), shape((layer, clusters, dof, dof), F32)],
        scratch_shapes=block_copies(2 * layer, clusters, dof) + [pltpu.SemaphoreType.DMA(())],
        compiler_params=params(16),
        cost_estimate=cost(10 * layer * dof * wres.size, 4 * layer * clusters * dof * dof),
    )(block_of, wres, wdisp, *fields)


def far_gradient(block_of, wdisp, rfar, far, prior):
    clusters, _, dof, _ = prior.shape
    layer = rfar.shape[0]
    hbm = pl.BlockSpec(memory_space=pltpu.HBM)
    return pl.pallas_call(
        far_gradient_kernel,
        in_specs=in_vmem(4) + [hbm],
        out_specs=hbm,
        out_shape=shape(prior.shape),
        scratch_shapes=block_copies(layer, clusters, dof)
        + [SMEM(block_of.shape, jnp.int32), pltpu.SemaphoreType.DMA(())],
        input_output_aliases={4: 0},
        compiler_params=params(8),
        cost_estimate=cost(2 * layer * dof * wdisp.size, 6 * layer * clusters * dof * dof),
    )(block_of, wdisp, rfar, far, prior)


def swap_near(block):
    count = lax.axis_size("cx")
    return lax.ppermute(block, "cx", [(i, i ^ 1) for i in range(count)])


def swap_far(block):
    count = lax.axis_size("cx")
    pairs = [(i, (i + 1) % count if i % 2 else (i - 1) % count) for i in range(count)]
    return lax.ppermute(block, "cx", pairs)


def far_of(i, count):
    return (i + 2 * (i % 2) - 1) % count


def routes(position, width, reach):
    q = lax.broadcasted_iota(jnp.int32, (8, 128), 1)
    row = lax.broadcasted_iota(jnp.int32, (8, 128), 0)
    peer = position ^ q
    who = jnp.where(row == 4, far_of(position, width), position)
    flag = (who < reach).astype(jnp.int32)
    return jnp.where(row == 0, far_of(peer, width), jnp.where(row == 1, peer, flag))


def arrange(field, atom_map):
    taken = jnp.take(field, atom_map.reshape(-1), axis=2)
    taken = taken.reshape(field.shape[0], 3, atom_map.shape[0], atom_map.shape[1])
    return jnp.transpose(taken, (2, 1, 3, 0)).reshape(
        atom_map.shape[0], 3 * atom_map.shape[1], field.shape[0]
    )


def tables(neighbours, config_order, weights, layer, position, width):
    blocks = neighbours.shape[1]
    offset = (neighbours // layer - position + 1 + width) % width
    partner = jnp.where(position % 2 == 0, 2, 0)
    group = jnp.where(offset == 1, 0, jnp.where(offset == partner, 1, 2))
    slot = group * layer + neighbours % layer
    named = slot[:, None, :] == jnp.arange(3 * layer, dtype=jnp.int32)[None, :, None]
    block_of = jnp.min(
        jnp.where(named, jnp.arange(blocks, dtype=jnp.int32)[None, None, :], blocks), axis=2
    )
    match = config_order[:, None] == jnp.arange(config_order.shape[0], dtype=jnp.int32)[None, :]
    wt = jnp.sum(jnp.where(match, weights[None, :], 0.0), axis=1)[None, :]
    return block_of, wt


def shards(displacements, forces, phi, neighbours, cluster_atoms, config_order, weights):
    width = lax.axis_size("cx")
    position = lax.axis_index("cx")
    layer, atoms = cluster_atoms.shape
    per = displacements.shape[2] // width
    block_of, wt = tables(neighbours, config_order, weights, layer, position, width)
    atom_local = cluster_atoms - position * per
    reach = width // 2
    dense = displacements.shape[0] % 16 == 0 and per % 128 == 64
    dense = dense and reach & (reach - 1) == 0 and displacements.shape[0] * reach % 128 == 0
    phi_far = ordered(block_of, phi)
    if dense:
        send = pack(
            jnp.transpose(displacements, (1, 0, 2)), jnp.transpose(forces, (1, 0, 2)), width
        )
        recv = lax.all_to_all(send, "cx", split_axis=0, concat_axis=0, tiled=True)
        index = (atom_local - 64 * (position % 2) + per) % per
        flags = routes(position, width, reach)
        index_far = swap_far(index).reshape(-1, 1)
        index = index.reshape(-1, 1)
        pieces = list(pick(flags, send, reach))
        for j in range(1, reach):
            pieces[j] = lax.ppermute(pieces[j], "cx", [(i, i ^ j) for i in range(width)])
        disp, passed = gather_and_pass(flags, index, recv, layer, atoms)
        recv_far = swap_far(passed)
        extra = (flags, index, recv, index_far, *pieces)
    else:
        disp, force = (
            arrange(lax.all_to_all(x, "cx", split_axis=2, concat_axis=0, tiled=True), atom_local)
            for x in (displacements, forces)
        )
        disp_far = swap_far(disp)
        extra = (force,)
    disp_near = swap_near(disp)
    base, wdisp, *direct = near_harmonic(block_of, phi, disp, disp_near, wt, dense, extra)
    if dense:
        res, wres, disp_far = merged_residual(
            flags, recv_far, direct[0], phi_far, base, wt
        )
    else:
        res, wres = residual_of(phi_far, disp_far, base, wt)
    res_far = swap_far(res)
    res_near = swap_near(res)
    gradient, residual, far = near_gradient(
        block_of, wres, wdisp, (disp, disp_near, disp_far, res, res_near), shape(phi.shape)
    )
    return residual, far_gradient(block_of, wdisp, res_far, far, gradient)


def solution(mesh):
    both = ("groups", "cx")
    in_specs = (
        P(both, None, None),
        P(both, None, None),
        P(both, None, None, None),
        P("cx", None),
        P("cx", None),
        P("groups"),
        P("groups"),
    )
    out_specs = (P(both, None, None), P(both, None, None, None))
    return jax.shard_map(shards, mesh=mesh, in_specs=in_specs, out_specs=out_specs, check_vma=False)
```
